512 devices in a mesh: pipe: 16 (over z), ctx: 32 (over y, x, core).
Axes of the slice: x: 4, y: 4, z: 16, core: 2. Of those that a mesh axis runs over, the one named last changes fastest.
Arguments:
- queries: bfloat16 [16, 4096, 1024], P('pipe', 'ctx'), may hold values from -80 to 80
- keys: bfloat16 [16, 4096, 128], P('pipe', 'ctx'), may hold values from -4 to 4
- values: bfloat16 [16, 4096, 128], P('pipe', 'ctx'), may hold values from -6 to 6
- attn_out: bfloat16 [16, 4096, 1024], P('pipe', 'ctx'), may hold values from -6 to 6
- grad_out: bfloat16 [16, 4096, 1024], P('pipe', 'ctx'), may hold values from -6 to 6
- doc_lengths: int32 [16], replicated, may hold values from 1 to 1024, 4096 in all
- pair_of_rank: int32 [32], replicated, may hold values from 0 to 31, each once
Outputs:
- query_grad: bfloat16 [16, 4096, 1024], P('pipe', 'ctx')
- handed_grad: bfloat16 [16, 4096, 1024], P('pipe', 'ctx')
- key_grad: bfloat16 [16, 4096, 128], P('pipe', 'ctx')
- value_grad: bfloat16 [16, 4096, 128], P('pipe', 'ctx')
The draws below stay inside these ranges and needn't reach their ends.
Inputs may be any that keep to these rules, and one draw needn't show every extreme that they name: `doc_lengths`: the lengths of the 16 documents packed in order into the 4096 positions; they sum to 4096, the same documents for every section. `pair_of_rank`: each stretch pair appears once; pair p is the stretches of positions p * 64 to (p + 1) * 64 - 1 and (63 - p) * 64 onwards.
All inputs are finite; a program needn't handle non-finite values.
Results may differ from the reference program's by a relative error of at most 0.015.
Values may be sent and summed in bfloat16 or wider, within the bound.
A program may use at most 64 MiB of HBM per device.

```python
import math
import jax
import jax.numpy as jnp
import numpy as np
from jax import lax

HQ = 8
HD = 128
CH = 64
NDOCS = 16
SECTIONS = 16
PAIRS = 32
SEQ = 4096
MOST = 1024
N_CTX = 32


def joint_draw(key):
    base = jax.random.fold_in(key, 7)
    raw_keys = jnp.clip(jax.random.normal(jax.random.fold_in(base, 1), (SECTIONS, SEQ, HD), jnp.float32), -4.0, 4.0)
    final_keys = raw_keys
    final_queries = jnp.clip(jax.random.normal(jax.random.fold_in(base, 2), (SECTIONS, SEQ, HQ * HD), jnp.float32), -4.0, 4.0)
    return (final_queries, final_keys)


def draw_queries(key, part):
    return joint_draw(key)[0].astype(jnp.bfloat16)


def draw_keys(key, part):
    return joint_draw(key)[1].astype(jnp.bfloat16)


def level_of(key, dims, pieces, smallest, high):
    def one(dim, parts):
        heights = jax.random.uniform(jax.random.fold_in(jax.random.fold_in(key, 6), dim), (parts,), jnp.float32, smallest / len(pieces), high / len(pieces))
        return jnp.repeat(jnp.exp(heights), dims[dim] // parts).reshape((-1,) + (1,) * (len(dims) - dim - 1))

    gain = one(*pieces[0])
    for cut in pieces[1:]:
        gain = gain * one(*cut)
    return gain


def profile(amount, total, reach, lean):
    loads = [(1 << 20) // math.isqrt(grade ** lean) + 1 for grade in range(2, amount + 1)]
    surplus, given = total - reach - (amount - 1), [1] * (amount - 1)
    while surplus > 0:
        free = [i for i in range(amount - 1) if given[i] < reach]
        whole, budget = sum([loads[i] for i in free]), surplus
        for i in free:
            addition = min(reach - given[i], max(1, budget * loads[i] // whole), surplus)
            given[i] = given[i] + addition
            surplus = surplus - addition
    return np.array([reach] + given)


def ragged_sizes(stream_key, number_of, total, reach, lean):
    if number_of == 2:
        one = jax.random.randint(stream_key, (), max(1, total - reach), min(reach, total - 1) + 1)
        return jnp.stack([one, total - one])
    sizes = jnp.asarray(profile(number_of, total, reach, lean), jnp.int32)
    pairs = (number_of - 1) // 2
    giver, taker = sizes[1:1 + 2 * pairs:2], sizes[2:2 + 2 * pairs:2]
    room = jnp.minimum(giver - 1, reach - taker)
    moved = jax.random.randint(jax.random.fold_in(stream_key, 1), (pairs,), 0, 1 << 20) % (room + 1)
    sizes = sizes.at[1:1 + 2 * pairs:2].set(giver - moved).at[2:2 + 2 * pairs:2].set(taker + moved)
    return sizes[jax.random.permutation(jax.random.fold_in(stream_key, 2), number_of)]


def noise(key, shape, width, most, cuts=(), kind=jnp.bfloat16):
    result = width * jax.random.normal(key, shape, jnp.float32)
    if cuts:
        result = result * level_of(key, shape, cuts, -0.22, 0.18)
    return jnp.clip(result, -most, most).astype(kind)


def setup_inputs(seed: int = 0) -> dict:
    key_list = jax.random.split(jax.random.key(seed), 8)
    queries = draw_queries(jax.random.fold_in(key_list[7], 71), 0)
    keys = draw_keys(jax.random.fold_in(key_list[7], 71), 0)
    values = noise(key_list[2], (SECTIONS, SEQ, HD), 1.0, 6.0, ((0, 16), (1, 32)))
    attn_out = noise(key_list[3], (SECTIONS, SEQ, HQ * HD), 1.0, 6.0, ((0, 16), (1, 32)))
    grad_out = noise(key_list[4], (SECTIONS, SEQ, HQ * HD), 1.0, 6.0, ((0, 16), (1, 32)))
    doc_lengths = ragged_sizes(key_list[5], NDOCS, SEQ, MOST, 2).astype(jnp.int32)
    pair_of_rank = jax.random.permutation(key_list[6], PAIRS).astype(jnp.int32)
    return {"queries": queries, "keys": keys, "values": values, "attn_out": attn_out, "grad_out": grad_out, "doc_lengths": doc_lengths, "pair_of_rank": pair_of_rank}


def seq_positions(pair_of_rank):
    rows = jnp.arange(SEQ, dtype=jnp.int32)
    span = 2 * CH
    ranks = rows // span
    within = rows % span
    match = ranks[:, None] == jnp.arange(N_CTX, dtype=jnp.int32)[None, :]
    pairs = lax.optimization_barrier(jnp.sum(jnp.where(match, pair_of_rank[None, :], 0), axis=1)).astype(jnp.int32)
    early = pairs * CH + within
    late = (2 * N_CTX - 1 - pairs) * CH + within - CH
    return jnp.where(within < CH, early, late).astype(jnp.int32)

def seq_documents(positions, doc_lengths):
    ends = jnp.cumsum(doc_lengths).astype(jnp.int32)
    return lax.optimization_barrier(jnp.sum((positions[:, None] >= ends[None, :]).astype(jnp.int32), axis=1)).astype(jnp.int32)

def reference(queries, keys, values, attn_out, grad_out, doc_lengths, pair_of_rank):
    scale = 1.0 / math.sqrt(HD)
    tok = 2 * CH
    position = seq_positions(pair_of_rank)
    document = seq_documents(position, doc_lengths)

    def section(operands):
        section_q, section_k, section_v, section_o, section_g = operands
        key_full = section_k.astype(jnp.float32)
        value_full = section_v.astype(jnp.float32)

        def per_rank(carry, rank):
            key_sum, value_sum = carry
            start = (rank * tok).astype(jnp.int32)
            query_heads = lax.dynamic_slice_in_dim(section_q, start, tok, 0).astype(jnp.float32).reshape(tok, HQ, HD)
            out_heads = lax.dynamic_slice_in_dim(section_o, start, tok, 0).astype(jnp.float32).reshape(tok, HQ, HD)
            grad_heads = lax.dynamic_slice_in_dim(section_g, start, tok, 0).astype(jnp.float32).reshape(tok, HQ, HD)
            own_pos = lax.dynamic_slice_in_dim(position, start, tok, 0)
            own_doc = lax.dynamic_slice_in_dim(document, start, tok, 0)
            allowed = (own_doc[:, None] == document[None, :]) & (position[None, :] <= own_pos[:, None])
            scores = jnp.einsum('qhd,kd->hqk', query_heads, key_full) * scale
            masked = jnp.where(allowed[None], scores, -jnp.inf)
            lse = jax.scipy.special.logsumexp(masked, axis=2)
            probs = jnp.where(allowed[None], jnp.exp(scores - lse[:, :, None]), 0.0)
            probs_low = probs.astype(jnp.bfloat16).astype(jnp.float32)
            dprobs = jnp.einsum('qhd,kd->hqk', grad_heads, value_full)
            delta = jnp.einsum('qhd,qhd->hq', grad_heads, out_heads)
            dscores = (probs * (dprobs - delta[:, :, None])).astype(jnp.bfloat16).astype(jnp.float32)
            dquery = jnp.einsum('hqk,kd->qhd', dscores, key_full) * scale
            key_part = jnp.einsum('hqk,qhd->kd', dscores, query_heads) * scale
            value_part = jnp.einsum('hqk,qhd->kd', probs_low, grad_heads)
            key_part = lax.optimization_barrier(key_part.astype(jnp.bfloat16)).astype(jnp.float32)
            value_part = lax.optimization_barrier(value_part.astype(jnp.bfloat16)).astype(jnp.float32)
            return ((key_sum + key_part, value_sum + value_part), dquery.reshape(tok, HQ * HD).astype(jnp.bfloat16))
        empty = jnp.zeros((SEQ, HD), jnp.float32)
        sums, dquery_all = lax.scan(per_rank, (empty, empty), jnp.arange(N_CTX, dtype=jnp.int32))
        return (dquery_all.reshape(SEQ, HQ * HD), sums[0].astype(jnp.bfloat16), sums[1].astype(jnp.bfloat16))
    query_grad, key_grad, value_grad = lax.map(section, (queries, keys, values, attn_out, grad_out))
    handed_grad = jnp.roll(query_grad, -1, axis=0)
    return (query_grad, handed_grad, key_grad, value_grad)
```

```python
import math

import jax
import jax.numpy as jnp
from jax import lax
from jax.experimental import pallas as pl
from jax.experimental.pallas import tpu as pltpu
from jax.sharding import PartitionSpec as P

HQ = 8
HD = 128
ST = 64
RANKS = 32
SIDE = 4
STRETCHES = 2 * RANKS
WIN = 18
CHUNK = 384
CHUNKS = WIN * ST // CHUNK
ROWS = HQ * ST
GROUP = 2 * SIDE
NEG = -1e30
MESH = pl.DeviceIdType.MESH
F32 = jnp.float32
BF16 = jnp.bfloat16


class Place:
    def __init__(self):
        me = lax.axis_index("ctx")
        self.core = lax.rem(me, 2)
        chip = me // 2
        self.x = lax.rem(chip, SIDE)
        self.y = chip // SIDE

    def at(self, dx, dy):
        x = lax.rem(self.x + dx + SIDE, SIDE)
        y = lax.rem(self.y + dy + SIDE, SIDE)
        return (y * SIDE + x) * 2 + self.core

    def sibling(self):
        return (self.y * SIDE + self.x) * 2 + 1 - self.core

    def neighbours(self):
        return [self.sibling(), self.at(1, 0), self.at(-1, 0), self.at(0, 1), self.at(0, -1)]

    def order(self, fast_is_x):
        if fast_is_x:
            return self.x, self.y, (lambda d: self.at(d, 0)), (lambda d: self.at(0, d))
        return self.y, self.x, (lambda d: self.at(0, d)), (lambda d: self.at(d, 0))


def step(i, d):
    return lax.rem(i + d + SIDE, SIDE)


def in_turn(*streams):
    live = list(streams)
    while live:
        for stream in list(live):
            if next(stream, StopIteration) is StopIteration:
                live.remove(stream)


def sender(send_sem, recv_sem):
    sent = {}

    def send(i, src, dst, device):
        copy = pltpu.make_async_remote_copy(
            src_ref=src, dst_ref=dst, send_sem=send_sem.at[i], recv_sem=recv_sem.at[i],
            device_id={"ctx": device}, device_id_type=MESH,
        )
        copy.start()
        sent[i] = copy

    return sent, send


def gather_stream(place, fast_is_x, own, full, own_sem, send_sem, recv_sem):
    fast, slow, along_fast, along_slow = place.order(fast_is_x)
    sent, send = sender(send_sem, recv_sem)
    half = place.core * (SIDE * GROUP)

    def block(d, lo=0, n=2):
        return full.at[pl.ds(half + slow * GROUP + step(fast, d) * 2 + lo, n)]

    def group(d, lo=0, n=GROUP):
        return full.at[pl.ds(half + step(slow, d) * GROUP + lo, n)]

    send(0, own, block(0), along_fast(1))
    send(1, own, block(0), along_fast(-1))
    mine = pltpu.make_async_copy(own, block(0), own_sem)
    mine.start()
    yield
    sent[0].wait_recv()
    send(2, block(-1, 0, 1), block(-1, 0, 1), along_fast(1))
    yield
    sent[1].wait_recv()
    send(3, block(1, 1, 1), block(1, 1, 1), along_fast(-1))
    mine.wait()
    yield
    sent[2].wait_recv()
    sent[3].wait_recv()
    send(4, group(0), group(0), along_slow(1))
    send(5, group(0), group(0), along_slow(-1))
    send(6, group(0), group(0), place.sibling())
    yield
    sent[4].wait_recv()
    send(7, group(-1, 0, SIDE), group(-1, 0, SIDE), along_slow(1))
    send(9, group(-1), group(-1), place.sibling())
    yield
    sent[5].wait_recv()
    send(8, group(1, SIDE, SIDE), group(1, SIDE, SIDE), along_slow(-1))
    send(10, group(1), group(1), place.sibling())
    yield
    sent[7].wait_recv()
    sent[8].wait_recv()
    send(11, group(2), group(2), place.sibling())
    yield
    for i in (6, 9, 10, 11):
        sent[i].wait_recv()
    for i in range(12):
        sent[i].wait_send()


def gather_kernel(k_ref, v_ref, gk_ref, gv_ref, own_sem, k_send, k_recv, v_send, v_recv):
    place = Place()
    barrier = pltpu.get_barrier_semaphore()
    for device in place.neighbours():
        pl.semaphore_signal(barrier, inc=1, device_id={"ctx": device}, device_id_type=MESH)
    pl.semaphore_wait(barrier, 5)
    in_turn(
        gather_stream(place, True, k_ref, gk_ref, own_sem.at[0], k_send, k_recv),
        gather_stream(place, False, v_ref, gv_ref, own_sem.at[1], v_send, v_recv),
    )


def add(*terms):
    total = terms[0].astype(F32)
    for term in terms[1:]:
        total = total + term.astype(F32)
    return total.astype(BF16)


def scatter_stream(place, fast_is_x, part, out, bufs, send_sem, recv_sem):
    sib, acc, across_a, across_b, from_low, from_high, line, near_a, near_b, end_low, end_high = bufs
    fast, slow, along_fast, along_slow = place.order(fast_is_x)
    sent, send = sender(send_sem, recv_sem)
    mine, other = place.core * (SIDE * GROUP), (1 - place.core) * (SIDE * GROUP)

    def at(d, lo=0, n=GROUP):
        return pl.ds(step(slow, d) * GROUP + lo, n)

    def merge(d):
        acc[at(d)] = add(part[pl.ds(mine + step(slow, d) * GROUP, GROUP)], sib[at(d)])

    for i, d in enumerate((2, 1, -1, 0)):
        send(i, part.at[pl.ds(other + step(slow, d) * GROUP, GROUP)], sib.at[at(d)], place.sibling())
    yield
    sent[0].wait_recv()
    merge(2)
    send(4, acc.at[at(2, 0, SIDE)], across_a, along_slow(1))
    send(5, acc.at[at(2, SIDE, SIDE)], across_b, along_slow(-1))
    yield
    sent[1].wait_recv()
    merge(1)
    send(6, acc.at[at(1, SIDE, SIDE)], from_low.at[pl.ds(SIDE, SIDE)], along_slow(1))
    yield
    sent[2].wait_recv()
    merge(-1)
    send(7, acc.at[at(-1, 0, SIDE)], from_high.at[pl.ds(0, SIDE)], along_slow(-1))
    yield
    sent[3].wait_recv()
    merge(0)
    yield
    sent[4].wait_recv()
    acc[at(1, 0, SIDE)] = add(acc[at(1, 0, SIDE)], across_a[...])
    send(8, acc.at[at(1, 0, SIDE)], from_low.at[pl.ds(0, SIDE)], along_slow(1))
    yield
    sent[5].wait_recv()
    acc[at(-1, SIDE, SIDE)] = add(acc[at(-1, SIDE, SIDE)], across_b[...])
    send(9, acc.at[at(-1, SIDE, SIDE)], from_high.at[pl.ds(SIDE, SIDE)], along_slow(-1))
    yield
    for i in (6, 7, 8, 9):
        sent[i].wait_recv()
    line[...] = add(acc[at(0)], from_low[...], from_high[...])

    def one(d, lo, n=1):
        return pl.ds(step(fast, d) * 2 + lo, n)

    send(10, line.at[one(2, 0)], near_a, along_fast(1))
    send(11, line.at[one(2, 1)], near_b, along_fast(-1))
    send(12, line.at[one(1, 1)], end_low.at[pl.ds(1, 1)], along_fast(1))
    send(13, line.at[one(-1, 0)], end_high.at[pl.ds(0, 1)], along_fast(-1))
    yield
    sent[10].wait_recv()
    line[one(1, 0)] = add(line[one(1, 0)], near_a[...])
    send(14, line.at[one(1, 0)], end_low.at[pl.ds(0, 1)], along_fast(1))
    yield
    sent[11].wait_recv()
    line[one(-1, 1)] = add(line[one(-1, 1)], near_b[...])
    send(15, line.at[one(-1, 1)], end_high.at[pl.ds(1, 1)], along_fast(-1))
    yield
    for i in (12, 13, 14, 15):
        sent[i].wait_recv()
    out[...] = add(line[one(0, 0, 2)], end_low[...], end_high[...])
    for i in range(16):
        sent[i].wait_send()


SCATTER_BUFS = (SIDE * GROUP, SIDE * GROUP, SIDE, SIDE, GROUP, GROUP, GROUP, 1, 1, 2, 2)


def scatter_kernel(kp_ref, vp_ref, dq_ref, kg_ref, vg_ref, handed_ref, *scratch):
    count = len(SCATTER_BUFS)
    k_bufs, v_bufs = scratch[:count], scratch[count : 2 * count]
    k_send, k_recv, v_send, v_recv, hand_sem = scratch[2 * count :]
    place = Place()
    section, sections = lax.axis_index("pipe"), lax.axis_size("pipe")
    below = lax.rem(section + sections - 1, sections)
    above = lax.rem(section + 1, sections)
    barrier = pltpu.get_barrier_semaphore()
    for device in place.neighbours():
        pl.semaphore_signal(barrier, inc=1, device_id={"ctx": device}, device_id_type=MESH)
    for device in (below, above):
        pl.semaphore_signal(barrier, inc=1, device_id={"pipe": device}, device_id_type=MESH)
    pl.semaphore_wait(barrier, 7)
    hand = pltpu.make_async_remote_copy(
        src_ref=dq_ref, dst_ref=handed_ref, send_sem=hand_sem.at[0], recv_sem=hand_sem.at[1],
        device_id={"pipe": below}, device_id_type=MESH,
    )
    hand.start()
    in_turn(
        scatter_stream(place, True, kp_ref, kg_ref, k_bufs, k_send, k_recv),
        scatter_stream(place, False, vp_ref, vg_ref, v_bufs, v_send, v_recv),
    )
    hand.wait()


def dot(a, b, over):
    return lax.dot_general(a, b, ((over[:1], over[1:]), ((), ())), preferred_element_type=F32)


def attend_kernel(
    docs, pairs, q_ref, o_ref, g_ref, k_ref, v_ref, dq_ref, kp_ref, vp_ref,
    rank_of_pair, q_rows, g_rows, key_win, value_win, work, key_terms, value_terms,
):
    scale = 1.0 / math.sqrt(HD)
    pair = pairs[lax.axis_index("ctx")]

    def note(r, carry):
        rank_of_pair[pairs[r]] = r
        return carry

    lax.fori_loop(0, RANKS, note, 0)

    def places(t):
        late = (t >= RANKS).astype(jnp.int32)
        rank = rank_of_pair[jnp.where(t >= RANKS, STRETCHES - 1 - t, t)]
        core, chip = lax.rem(rank, 2), rank // 2
        turned = lax.rem(chip, SIDE) * SIDE + chip // SIDE
        size = SIDE * SIDE
        return (core * size + chip) * 2 + late, (core * size + turned) * 2 + late

    kp_ref[...] = jnp.zeros_like(kp_ref)
    vp_ref[...] = jnp.zeros_like(vp_ref)
    bases = (pair, STRETCHES - 1 - pair)
    lane = lax.rem(lax.broadcasted_iota(jnp.int32, (1, ROWS), 1), ST)
    for which in range(2):
        base = bases[which]
        lowest = (base - (WIN - 1)) * ST
        rows = slice(which * ST, (which + 1) * ST)
        for h in range(HQ):
            q_rows[h * ST : (h + 1) * ST] = q_ref[rows, h * HD : (h + 1) * HD]
            g_rows[h * ST : (h + 1) * ST] = g_ref[rows, h * HD : (h + 1) * HD]
        products = jnp.concatenate(
            [
                g_ref[rows, h * HD : (h + 1) * HD].astype(F32) * o_ref[rows, h * HD : (h + 1) * HD].astype(F32)
                for h in range(HQ)
            ],
            axis=0,
        )
        delta = jnp.sum(jnp.transpose(products), axis=0, keepdims=True)
        for j in range(WIN):
            k_at, v_at = places(jnp.maximum(base - (WIN - 1) + j, 0))
            key_win[j * ST : (j + 1) * ST] = k_ref[k_at]
            value_win[j * ST : (j + 1) * ST] = v_ref[v_at]
        position = base * ST + lane
        start, first, end = jnp.zeros_like(position), jnp.int32(0), jnp.int32(0)
        for d in range(docs.shape[0]):
            end = end + docs[d]
            start = jnp.where(position >= end, end, start)
            first = jnp.where(base * ST >= end, end, first)
        low, high = start - lowest, position - lowest
        begin = (first - lowest) // CHUNK

        def scores(c, top):
            at = pl.multiple_of(c * CHUNK, CHUNK)
            found = dot(key_win[pl.ds(at, CHUNK)], q_rows[...], (1, 1))
            where = lax.broadcasted_iota(jnp.int32, (CHUNK, ROWS), 0) + at
            found = jnp.where((where >= low) & (where <= high), found, NEG)
            work[c] = found
            return jnp.maximum(top, jnp.max(found, axis=0, keepdims=True))

        top = lax.fori_loop(begin, CHUNKS, scores, jnp.full((1, ROWS), NEG, F32))

        def weigh(c, total):
            weights = jnp.exp2((work[c] - top) * (scale * math.log2(math.e)))
            work[c] = weights
            return total + jnp.sum(weights, axis=0, keepdims=True)

        total = lax.fori_loop(begin, CHUNKS, weigh, jnp.zeros((1, ROWS), F32))
        inverse = 1.0 / total

        def grads(c, dq_sum):
            at = pl.multiple_of(c * CHUNK, CHUNK)
            probs = work[c] * inverse
            value_terms[which, pl.ds(at, CHUNK)] = dot(probs.astype(BF16), g_rows[...], (1, 0))
            dprobs = dot(value_win[pl.ds(at, CHUNK)], g_rows[...], (1, 1))
            dscores = (probs * (dprobs - delta)).astype(BF16)
            key_terms[which, pl.ds(at, CHUNK)] = dot(dscores, q_rows[...], (1, 0)) * scale
            turned = jnp.transpose(key_win[pl.ds(at, CHUNK)])
            return dq_sum + dot(turned, dscores, (1, 0))

        dq_sum = lax.fori_loop(begin, CHUNKS, grads, jnp.zeros((HD, ROWS), F32))
        dq_rows = (jnp.transpose(dq_sum) * scale).astype(BF16)
        for h in range(HQ):
            dq_ref[rows, h * HD : (h + 1) * HD] = dq_rows[h * ST : (h + 1) * ST]

        def clear(c, carry):
            at = pl.multiple_of(c * CHUNK, CHUNK)
            key_terms[which, pl.ds(at, CHUNK)] = jnp.zeros((CHUNK, HD), F32)
            value_terms[which, pl.ds(at, CHUNK)] = jnp.zeros((CHUNK, HD), F32)
            return carry

        lax.fori_loop(0, begin, clear, 0)

    early, late = bases[0] - (WIN - 1), bases[1] - (WIN - 1)

    def put_early(j, carry):
        t = early + j

        @pl.when((t >= 0) & (t < late))
        def _():
            k_at, v_at = places(t)
            at = pl.multiple_of(j * ST, ST)
            kp_ref[k_at] = key_terms[0, pl.ds(at, ST)].astype(BF16)
            vp_ref[v_at] = value_terms[0, pl.ds(at, ST)].astype(BF16)

        return carry

    lax.fori_loop(0, WIN, put_early, 0)

    def put_late(j, carry):
        t = late + j
        k_at, v_at = places(t)
        at = pl.multiple_of(j * ST, ST)
        shared = t - early
        both = (shared >= 0) & (shared < WIN)
        near = pl.multiple_of(jnp.clip(shared, 0, WIN - 1) * ST, ST)
        kp_ref[k_at] = (
            key_terms[1, pl.ds(at, ST)] + jnp.where(both, key_terms[0, pl.ds(near, ST)], 0.0)
        ).astype(BF16)
        vp_ref[v_at] = (
            value_terms[1, pl.ds(at, ST)] + jnp.where(both, value_terms[0, pl.ds(near, ST)], 0.0)
        ).astype(BF16)
        return carry

    lax.fori_loop(0, WIN, put_late, 0)


def on_device(queries, keys, values, attn_out, grad_out, doc_lengths, pair_of_rank):
    vmem = pl.BlockSpec(memory_space=pltpu.VMEM)
    smem = pl.BlockSpec(memory_space=pltpu.SMEM)
    hbm = pl.BlockSpec(memory_space=pl.ANY)
    full = jax.ShapeDtypeStruct((STRETCHES, ST, HD), BF16)
    own = jax.ShapeDtypeStruct((2, ST, HD), BF16)
    tok = 2 * ST
    dma = pltpu.SemaphoreType.DMA
    all_keys, all_values = pl.pallas_call(
        gather_kernel,
        out_shape=(full, full),
        in_specs=[vmem] * 2,
        out_specs=(vmem, vmem),
        scratch_shapes=[dma((2,)), dma((12,)), dma((12,)), dma((12,)), dma((12,))],
        compiler_params=pltpu.CompilerParams(collective_id=0, has_side_effects=True),
        name="gather_keys_values",
    )(keys.reshape(2, ST, HD), values.reshape(2, ST, HD))
    query_grad, key_part, value_part = pl.pallas_call(
        attend_kernel,
        out_shape=(jax.ShapeDtypeStruct((tok, HQ * HD), BF16), full, full),
        in_specs=[smem] * 2 + [vmem] * 5,
        out_specs=(vmem,) * 3,
        scratch_shapes=[
            pltpu.SMEM((RANKS,), jnp.int32),
            pltpu.VMEM((ROWS, HD), BF16),
            pltpu.VMEM((ROWS, HD), BF16),
            pltpu.VMEM((WIN * ST, HD), BF16),
            pltpu.VMEM((WIN * ST, HD), BF16),
            pltpu.VMEM((CHUNKS, CHUNK, ROWS), F32),
            pltpu.VMEM((2, WIN * ST, HD), F32),
            pltpu.VMEM((2, WIN * ST, HD), F32),
        ],
        name="attend_backward",
    )(doc_lengths, pair_of_rank, queries[0], attn_out[0], grad_out[0], all_keys, all_values)
    bufs = [pltpu.VMEM((n, ST, HD), BF16) for n in SCATTER_BUFS]
    key_grad, value_grad, handed = pl.pallas_call(
        scatter_kernel,
        out_shape=(own, own, jax.ShapeDtypeStruct((tok, HQ * HD), BF16)),
        in_specs=[vmem, vmem, hbm],
        out_specs=(vmem, vmem, hbm),
        scratch_shapes=bufs + bufs + [dma((16,)), dma((16,)), dma((16,)), dma((16,)), dma((2,))],
        compiler_params=pltpu.CompilerParams(collective_id=1, has_side_effects=True),
        name="scatter_grads",
    )(key_part, value_part, query_grad)
    return (
        query_grad[None],
        handed[None],
        key_grad.reshape(1, tok, HD),
        value_grad.reshape(1, tok, HD),
    )


def solution(mesh):
    split = P("pipe", "ctx", None)
    return jax.shard_map(
        on_device,
        mesh=mesh,
        in_specs=(split,) * 5 + (P(), P()),
        out_specs=(split,) * 4,
        check_vma=False,
    )
```

```python
import math

import jax
import jax.numpy as jnp
from jax import lax
from jax.experimental import pallas as pl
from jax.experimental.pallas import tpu as pltpu
from jax.sharding import PartitionSpec as P

HQ = 8
HD = 128
ST = 64
RANKS = 32
SIDE = 4
STRETCHES = 2 * RANKS
WIN = 18
CHUNK = 384
CHUNKS = WIN * ST // CHUNK
ROWS = HQ * ST
GROUP = 2 * SIDE
NEG = -1e30
MESH = pl.DeviceIdType.MESH
F32 = jnp.float32
BF16 = jnp.bfloat16


class Place:
    def __init__(self):
        me = lax.axis_index("ctx")
        self.core = lax.rem(me, 2)
        chip = me // 2
        self.x = lax.rem(chip, SIDE)
        self.y = chip // SIDE

    def at(self, dx, dy):
        x = lax.rem(self.x + dx + SIDE, SIDE)
        y = lax.rem(self.y + dy + SIDE, SIDE)
        return (y * SIDE + x) * 2 + self.core

    def sibling(self):
        return (self.y * SIDE + self.x) * 2 + 1 - self.core

    def neighbours(self):
        return [self.sibling(), self.at(1, 0), self.at(-1, 0), self.at(0, 1), self.at(0, -1)]

    def order(self, fast_is_x):
        if fast_is_x:
            return self.x, self.y, (lambda d: self.at(d, 0)), (lambda d: self.at(0, d))
        return self.y, self.x, (lambda d: self.at(0, d)), (lambda d: self.at(d, 0))


def step(i, d):
    return lax.rem(i + d + SIDE, SIDE)


def in_turn(*streams):
    live = list(streams)
    while live:
        for stream in list(live):
            if next(stream, StopIteration) is StopIteration:
                live.remove(stream)


def sender(send_sem, recv_sem):
    sent = {}

    def send(i, src, dst, device):
        copy = pltpu.make_async_remote_copy(
            src_ref=src, dst_ref=dst, send_sem=send_sem.at[i], recv_sem=recv_sem.at[i],
            device_id={"ctx": device}, device_id_type=MESH,
        )
        copy.start()
        sent[i] = copy

    return sent, send


def gather_stream(place, fast_is_x, own, full, own_sem, send_sem, recv_sem):
    fast, slow, along_fast, along_slow = place.order(fast_is_x)
    sent, send = sender(send_sem, recv_sem)
    half = place.core * (SIDE * GROUP)

    def block(f, d=0, lo=0, n=2):
        return full.at[pl.ds(half + step(slow, d) * GROUP + step(fast, f) * 2 + lo, n)]

    def group(d):
        return full.at[pl.ds(half + step(slow, d) * GROUP, GROUP)]

    def spread(i, f, src=None):
        src = block(f) if src is None else src
        send(i, src, block(f), along_slow(1))
        send(i + 1, src, block(f), along_slow(-1))

    def relay(i, f, toward):
        send(i, block(f, -toward), block(f, -toward), along_slow(toward))

    send(0, own, block(0), along_fast(1))
    send(1, own, block(0), along_fast(-1))
    spread(4, 0, own)
    mine = pltpu.make_async_copy(own, block(0), own_sem)
    mine.start()
    yield
    sent[0].wait_recv()
    send(2, block(-1, 0, 0, 1), block(-1, 0, 0, 1), along_fast(1))
    spread(6, -1)
    yield
    sent[1].wait_recv()
    send(3, block(1, 0, 1, 1), block(1, 0, 1, 1), along_fast(-1))
    spread(8, 1)
    yield
    sent[4].wait_recv()
    relay(12, 0, 1)
    yield
    sent[2].wait_recv()
    sent[3].wait_recv()
    spread(10, 2)
    mine.wait()
    send(16, group(0), group(0), place.sibling())
    yield
    sent[7].wait_recv()
    relay(13, -1, -1)
    yield
    sent[9].wait_recv()
    relay(14, 1, -1)
    yield
    sent[10].wait_recv()
    relay(15, 2, 1)
    sent[6].wait_recv()
    sent[8].wait_recv()
    send(17, group(-1), group(-1), place.sibling())
    yield
    sent[5].wait_recv()
    sent[11].wait_recv()
    send(18, group(1), group(1), place.sibling())
    yield
    for n, f in enumerate((0, -1, 1, 2)):
        sent[12 + n].wait_recv()
        send(19 + n, block(f, 2), block(f, 2), place.sibling())
        yield
    for i in range(16, 23):
        sent[i].wait_recv()
    for i in range(23):
        sent[i].wait_send()


def gather_kernel(k_ref, v_ref, gk_ref, gv_ref, own_sem, k_send, k_recv, v_send, v_recv):
    place = Place()
    barrier = pltpu.get_barrier_semaphore()
    for device in place.neighbours():
        pl.semaphore_signal(barrier, inc=1, device_id={"ctx": device}, device_id_type=MESH)
    pl.semaphore_wait(barrier, 5)
    in_turn(
        gather_stream(place, True, k_ref, gk_ref, own_sem.at[0], k_send, k_recv),
        gather_stream(place, False, v_ref, gv_ref, own_sem.at[1], v_send, v_recv),
    )


def add(*terms):
    total = terms[0].astype(F32)
    for term in terms[1:]:
        total = total + term.astype(F32)
    return total.astype(BF16)


def scatter_stream(place, fast_is_x, part, out, bufs, send_sem, recv_sem):
    sib, acc, across, from_low, from_high, line, near_a, near_b, end_low, end_high = bufs
    fast, slow, along_fast, along_slow = place.order(fast_is_x)
    sent, send = sender(send_sem, recv_sem)
    mine, other = place.core * (SIDE * GROUP), (1 - place.core) * (SIDE * GROUP)
    order = (2, 1, -1, 0)
    way = (1, -1, -1, 1)

    def at(d):
        return pl.ds(step(slow, d) * GROUP, GROUP)

    def block(d, n):
        return pl.ds(step(slow, d) * GROUP + step(fast, order[n]) * 2, 2)

    def slot(n):
        return pl.ds(2 * n, 2)

    def merge(d):
        acc[at(d)] = add(part[pl.ds(mine + step(slow, d) * GROUP, GROUP)], sib[at(d)])

    for i, d in enumerate((2, 1, -1, 0)):
        send(i, part.at[pl.ds(other + step(slow, d) * GROUP, GROUP)], sib.at[at(d)], place.sibling())
    yield
    sent[0].wait_recv()
    merge(2)
    for n in range(4):
        send(4 + n, acc.at[block(2, n)], across.at[slot(n)], along_slow(way[n]))
    yield
    sent[1].wait_recv()
    merge(1)
    for n in (1, 2):
        send(8 + n, acc.at[block(1, n)], from_low.at[slot(n)], along_slow(1))
    yield
    sent[2].wait_recv()
    merge(-1)
    for n in (0, 3):
        send(8 + n, acc.at[block(-1, n)], from_high.at[slot(n)], along_slow(-1))
    yield
    sent[3].wait_recv()
    merge(0)
    yield
    for n in range(4):
        sent[4 + n].wait_recv()
        acc[block(way[n], n)] = add(acc[block(way[n], n)], across[slot(n)])
        target = from_low if way[n] == 1 else from_high
        send(12 + n, acc.at[block(way[n], n)], target.at[slot(n)], along_slow(way[n]))
        yield

    def settle(n):
        sent[8 + n].wait_recv()
        sent[12 + n].wait_recv()
        line[slot(n)] = add(acc[block(0, n)], from_low[slot(n)], from_high[slot(n)])

    settle(0)
    send(16, line.at[pl.ds(0, 1)], near_a, along_fast(1))
    send(17, line.at[pl.ds(1, 1)], near_b, along_fast(-1))
    yield
    settle(1)
    send(18, line.at[pl.ds(3, 1)], end_low.at[pl.ds(1, 1)], along_fast(1))
    yield
    settle(2)
    send(19, line.at[pl.ds(4, 1)], end_high.at[pl.ds(0, 1)], along_fast(-1))
    yield
    sent[16].wait_recv()
    line[pl.ds(2, 1)] = add(line[pl.ds(2, 1)], near_a[...])
    send(20, line.at[pl.ds(2, 1)], end_low.at[pl.ds(0, 1)], along_fast(1))
    yield
    sent[17].wait_recv()
    line[pl.ds(5, 1)] = add(line[pl.ds(5, 1)], near_b[...])
    send(21, line.at[pl.ds(5, 1)], end_high.at[pl.ds(1, 1)], along_fast(-1))
    yield
    settle(3)
    for i in (18, 19, 20, 21):
        sent[i].wait_recv()
    out[...] = add(line[slot(3)], end_low[...], end_high[...])
    for i in range(22):
        sent[i].wait_send()


SCATTER_BUFS = (SIDE * GROUP, SIDE * GROUP, GROUP, GROUP, GROUP, GROUP, 1, 1, 2, 2)


def scatter_kernel(kp_ref, vp_ref, kg_ref, vg_ref, *scratch):
    count = len(SCATTER_BUFS)
    k_bufs, v_bufs = scratch[:count], scratch[count : 2 * count]
    k_send, k_recv, v_send, v_recv = scratch[2 * count :]
    place = Place()
    barrier = pltpu.get_barrier_semaphore()
    for device in place.neighbours():
        pl.semaphore_signal(barrier, inc=1, device_id={"ctx": device}, device_id_type=MESH)
    pl.semaphore_wait(barrier, 5)
    in_turn(
        scatter_stream(place, True, kp_ref, kg_ref, k_bufs, k_send, k_recv),
        scatter_stream(place, False, vp_ref, vg_ref, v_bufs, v_send, v_recv),
    )


def dot(a, b, over):
    return lax.dot_general(a, b, ((over[:1], over[1:]), ((), ())), preferred_element_type=F32)


def attend_kernel(
    docs, pairs, q_ref, o_ref, g_ref, k_ref, v_ref, dq_ref, kp_ref, vp_ref,
    rank_of_pair, q_rows, g_rows, key_win, value_win, work, key_terms, value_terms,
):
    scale = 1.0 / math.sqrt(HD)
    pair = pairs[lax.axis_index("ctx")]

    def note(r, carry):
        rank_of_pair[pairs[r]] = r
        return carry

    lax.fori_loop(0, RANKS, note, 0)

    def places(t):
        late = (t >= RANKS).astype(jnp.int32)
        rank = rank_of_pair[jnp.where(t >= RANKS, STRETCHES - 1 - t, t)]
        core, chip = lax.rem(rank, 2), rank // 2
        turned = lax.rem(chip, SIDE) * SIDE + chip // SIDE
        size = SIDE * SIDE
        return (core * size + chip) * 2 + late, (core * size + turned) * 2 + late

    kp_ref[...] = jnp.zeros_like(kp_ref)
    vp_ref[...] = jnp.zeros_like(vp_ref)
    bases = (pair, STRETCHES - 1 - pair)
    lane = lax.rem(lax.broadcasted_iota(jnp.int32, (1, ROWS), 1), ST)
    for which in range(2):
        base = bases[which]
        lowest = (base - (WIN - 1)) * ST
        rows = slice(which * ST, (which + 1) * ST)
        for h in range(HQ):
            q_rows[h * ST : (h + 1) * ST] = q_ref[rows, h * HD : (h + 1) * HD]
            g_rows[h * ST : (h + 1) * ST] = g_ref[rows, h * HD : (h + 1) * HD]
        products = jnp.concatenate(
            [
                g_ref[rows, h * HD : (h + 1) * HD].astype(F32) * o_ref[rows, h * HD : (h + 1) * HD].astype(F32)
                for h in range(HQ)
            ],
            axis=0,
        )
        delta = jnp.sum(jnp.transpose(products), axis=0, keepdims=True)
        for j in range(WIN):
            k_at, v_at = places(jnp.maximum(base - (WIN - 1) + j, 0))
            key_win[j * ST : (j + 1) * ST] = k_ref[k_at]
            value_win[j * ST : (j + 1) * ST] = v_ref[v_at]
        position = base * ST + lane
        start, first, end = jnp.zeros_like(position), jnp.int32(0), jnp.int32(0)
        for d in range(docs.shape[0]):
            end = end + docs[d]
            start = jnp.where(position >= end, end, start)
            first = jnp.where(base * ST >= end, end, first)
        low, high = start - lowest, position - lowest
        begin = (first - lowest) // CHUNK

        def scores(c, top):
            at = pl.multiple_of(c * CHUNK, CHUNK)
            found = dot(key_win[pl.ds(at, CHUNK)], q_rows[...], (1, 1))
            where = lax.broadcasted_iota(jnp.int32, (CHUNK, ROWS), 0) + at
            found = jnp.where((where >= low) & (where <= high), found, NEG)
            work[c] = found
            return jnp.maximum(top, jnp.max(found, axis=0, keepdims=True))

        top = lax.fori_loop(begin, CHUNKS, scores, jnp.full((1, ROWS), NEG, F32))

        def weigh(c, total):
            weights = jnp.exp2((work[c] - top) * (scale * math.log2(math.e)))
            work[c] = weights
            return total + jnp.sum(weights, axis=0, keepdims=True)

        total = lax.fori_loop(begin, CHUNKS, weigh, jnp.zeros((1, ROWS), F32))
        inverse = 1.0 / total

        def grads(c, dq_sum):
            at = pl.multiple_of(c * CHUNK, CHUNK)
            probs = work[c] * inverse
            value_terms[which, pl.ds(at, CHUNK)] = dot(probs.astype(BF16), g_rows[...], (1, 0))
            dprobs = dot(value_win[pl.ds(at, CHUNK)], g_rows[...], (1, 1))
            dscores = (probs * (dprobs - delta)).astype(BF16)
            key_terms[which, pl.ds(at, CHUNK)] = dot(dscores, q_rows[...], (1, 0)) * scale
            turned = jnp.transpose(key_win[pl.ds(at, CHUNK)])
            return dq_sum + dot(turned, dscores, (1, 0))

        dq_sum = lax.fori_loop(begin, CHUNKS, grads, jnp.zeros((HD, ROWS), F32))
        dq_rows = (jnp.transpose(dq_sum) * scale).astype(BF16)
        for h in range(HQ):
            dq_ref[rows, h * HD : (h + 1) * HD] = dq_rows[h * ST : (h + 1) * ST]

        def clear(c, carry):
            at = pl.multiple_of(c * CHUNK, CHUNK)
            key_terms[which, pl.ds(at, CHUNK)] = jnp.zeros((CHUNK, HD), F32)
            value_terms[which, pl.ds(at, CHUNK)] = jnp.zeros((CHUNK, HD), F32)
            return carry

        lax.fori_loop(0, begin, clear, 0)

    early, late = bases[0] - (WIN - 1), bases[1] - (WIN - 1)

    def put_early(j, carry):
        t = early + j

        @pl.when((t >= 0) & (t < late))
        def _():
            k_at, v_at = places(t)
            at = pl.multiple_of(j * ST, ST)
            kp_ref[k_at] = key_terms[0, pl.ds(at, ST)].astype(BF16)
            vp_ref[v_at] = value_terms[0, pl.ds(at, ST)].astype(BF16)

        return carry

    lax.fori_loop(0, WIN, put_early, 0)

    def put_late(j, carry):
        t = late + j
        k_at, v_at = places(t)
        at = pl.multiple_of(j * ST, ST)
        shared = t - early
        both = (shared >= 0) & (shared < WIN)
        near = pl.multiple_of(jnp.clip(shared, 0, WIN - 1) * ST, ST)
        kp_ref[k_at] = (
            key_terms[1, pl.ds(at, ST)] + jnp.where(both, key_terms[0, pl.ds(near, ST)], 0.0)
        ).astype(BF16)
        vp_ref[v_at] = (
            value_terms[1, pl.ds(at, ST)] + jnp.where(both, value_terms[0, pl.ds(near, ST)], 0.0)
        ).astype(BF16)
        return carry

    lax.fori_loop(0, WIN, put_late, 0)


def on_device(queries, keys, values, attn_out, grad_out, doc_lengths, pair_of_rank):
    vmem = pl.BlockSpec(memory_space=pltpu.VMEM)
    smem = pl.BlockSpec(memory_space=pltpu.SMEM)
    hbm = pl.BlockSpec(memory_space=pl.ANY)
    full = jax.ShapeDtypeStruct((STRETCHES, ST, HD), BF16)
    own = jax.ShapeDtypeStruct((2, ST, HD), BF16)
    tok = 2 * ST
    dma = pltpu.SemaphoreType.DMA
    all_keys, all_values = pl.pallas_call(
        gather_kernel,
        out_shape=(full, full),
        in_specs=[vmem] * 2,
        out_specs=(vmem, vmem),
        scratch_shapes=[dma((2,))] + [dma((23,))] * 4,
        compiler_params=pltpu.CompilerParams(collective_id=0, has_side_effects=True),
        name="gather_keys_values",
    )(keys.reshape(2, ST, HD), values.reshape(2, ST, HD))
    query_grad, key_part, value_part = pl.pallas_call(
        attend_kernel,
        out_shape=(jax.ShapeDtypeStruct((tok, HQ * HD), BF16), full, full),
        in_specs=[smem] * 2 + [vmem] * 5,
        out_specs=(vmem,) * 3,
        scratch_shapes=[
            pltpu.SMEM((RANKS,), jnp.int32),
            pltpu.VMEM((ROWS, HD), BF16),
            pltpu.VMEM((ROWS, HD), BF16),
            pltpu.VMEM((WIN * ST, HD), BF16),
            pltpu.VMEM((WIN * ST, HD), BF16),
            pltpu.VMEM((CHUNKS, CHUNK, ROWS), F32),
            pltpu.VMEM((2, WIN * ST, HD), F32),
            pltpu.VMEM((2, WIN * ST, HD), F32),
        ],
        name="attend_backward",
    )(doc_lengths, pair_of_rank, queries[0], attn_out[0], grad_out[0], all_keys, all_values)
    bufs = [pltpu.VMEM((n, ST, HD), BF16) for n in SCATTER_BUFS]
    sections = lax.axis_size("pipe")
    handed = lax.ppermute(query_grad, "pipe", [(i, (i - 1) % sections) for i in range(sections)])
    key_grad, value_grad = pl.pallas_call(
        scatter_kernel,
        out_shape=(own, own),
        in_specs=[vmem] * 2,
        out_specs=(vmem,) * 2,
        scratch_shapes=bufs + bufs + [dma((22,))] * 4,
        compiler_params=pltpu.CompilerParams(collective_id=1, has_side_effects=True),
        cost_estimate=pl.CostEstimate(flops=2**30, bytes_accessed=2**26, transcendentals=0),
        name="scatter_grads",
    )(key_part, value_part)
    return (
        query_grad[None],
        handed[None],
        key_grad.reshape(1, tok, HD),
        value_grad.reshape(1, tok, HD),
    )


def solution(mesh):
    split = P("pipe", "ctx", None)
    return jax.shard_map(
        on_device,
        mesh=mesh,
        in_specs=(split,) * 5 + (P(), P()),
        out_specs=(split,) * 4,
        check_vma=False,
    )
```

```python
import math

import jax
import jax.numpy as jnp
from jax import lax
from jax.experimental import pallas as pl
from jax.experimental.pallas import tpu as pltpu
from jax.sharding import PartitionSpec as P

HQ = 8
HD = 128
ST = 64
RANKS = 32
SIDE = 4
STRETCHES = 2 * RANKS
WIN = 18
CHUNK = 384
PART = CHUNK // ST
CHUNKS = WIN * ST // CHUNK
ROWS = HQ * ST
GROUP = 2 * SIDE
NEG = -1e30
MESH = pl.DeviceIdType.MESH
F32 = jnp.float32
BF16 = jnp.bfloat16


class Place:
    def __init__(self):
        me = lax.axis_index("ctx")
        self.core = lax.rem(me, 2)
        chip = me // 2
        self.x = lax.rem(chip, SIDE)
        self.y = chip // SIDE

    def at(self, dx, dy):
        x = lax.rem(self.x + dx + SIDE, SIDE)
        y = lax.rem(self.y + dy + SIDE, SIDE)
        return (y * SIDE + x) * 2 + self.core

    def sibling(self):
        return (self.y * SIDE + self.x) * 2 + 1 - self.core

    def neighbours(self):
        return [self.sibling(), self.at(1, 0), self.at(-1, 0), self.at(0, 1), self.at(0, -1)]

    def order(self, fast_is_x):
        if fast_is_x:
            return self.x, self.y, (lambda d: self.at(d, 0)), (lambda d: self.at(0, d))
        return self.y, self.x, (lambda d: self.at(0, d)), (lambda d: self.at(d, 0))


def step(i, d):
    return lax.rem(i + d + SIDE, SIDE)


def in_turn(*streams):
    live = list(streams)
    while live:
        for stream in list(live):
            if next(stream, StopIteration) is StopIteration:
                live.remove(stream)


def sender(send_sem, recv_sem):
    sent = {}

    def send(i, src, dst, device):
        copy = pltpu.make_async_remote_copy(
            src_ref=src, dst_ref=dst, send_sem=send_sem.at[i], recv_sem=recv_sem.at[i],
            device_id={"ctx": device}, device_id_type=MESH,
        )
        copy.start()
        sent[i] = copy

    return sent, send


def gather_stream(place, fast_is_x, own, full, own_sem, send_sem, recv_sem):
    fast, slow, along_fast, along_slow = place.order(fast_is_x)
    sent, send = sender(send_sem, recv_sem)
    half = place.core * (SIDE * GROUP)

    def block(f, d=0, lo=0, n=2):
        return full.at[pl.ds(half + step(slow, d) * GROUP + step(fast, f) * 2 + lo, n)]

    def group(d):
        return full.at[pl.ds(half + step(slow, d) * GROUP, GROUP)]

    def spread(i, f, src=None):
        src = block(f) if src is None else src
        send(i, src, block(f), along_slow(1))
        send(i + 1, src, block(f), along_slow(-1))

    def relay(i, f, toward):
        send(i, block(f, -toward), block(f, -toward), along_slow(toward))

    send(0, own, block(0), along_fast(1))
    send(1, own, block(0), along_fast(-1))
    spread(4, 0, own)
    mine = pltpu.make_async_copy(own, block(0), own_sem)
    mine.start()
    yield
    sent[0].wait_recv()
    send(2, block(-1, 0, 0, 1), block(-1, 0, 0, 1), along_fast(1))
    spread(6, -1)
    yield
    sent[1].wait_recv()
    send(3, block(1, 0, 1, 1), block(1, 0, 1, 1), along_fast(-1))
    spread(8, 1)
    yield
    sent[4].wait_recv()
    relay(12, 0, 1)
    yield
    sent[2].wait_recv()
    sent[3].wait_recv()
    spread(10, 2)
    mine.wait()
    send(16, group(0), group(0), place.sibling())
    yield
    sent[7].wait_recv()
    relay(13, -1, -1)
    yield
    sent[9].wait_recv()
    relay(14, 1, -1)
    yield
    sent[10].wait_recv()
    relay(15, 2, 1)
    sent[6].wait_recv()
    sent[8].wait_recv()
    send(17, group(-1), group(-1), place.sibling())
    yield
    sent[5].wait_recv()
    sent[11].wait_recv()
    send(18, group(1), group(1), place.sibling())
    yield
    for n, f in enumerate((0, -1, 1, 2)):
        sent[12 + n].wait_recv()
        send(19 + n, block(f, 2), block(f, 2), place.sibling())
        yield
    for i in range(16, 23):
        sent[i].wait_recv()
    for i in range(23):
        sent[i].wait_send()


def gather_kernel(k_ref, v_ref, gk_ref, gv_ref, own_sem, k_send, k_recv, v_send, v_recv):
    place = Place()
    barrier = pltpu.get_barrier_semaphore()
    for device in place.neighbours():
        pl.semaphore_signal(barrier, inc=1, device_id={"ctx": device}, device_id_type=MESH)
    pl.semaphore_wait(barrier, 5)
    in_turn(
        gather_stream(place, True, k_ref, gk_ref, own_sem.at[0], k_send, k_recv),
        gather_stream(place, False, v_ref, gv_ref, own_sem.at[1], v_send, v_recv),
    )


def add(*terms):
    total = terms[0].astype(F32)
    for term in terms[1:]:
        total = total + term.astype(F32)
    return total.astype(BF16)


def scatter_stream(place, fast_is_x, term, out, bufs, send_sem, recv_sem):
    outgoing, sib, acc, across, from_low, from_high, line, near_a, near_b, end_low, end_high = bufs
    fast, slow, along_fast, along_slow = place.order(fast_is_x)
    sent, send = sender(send_sem, recv_sem)
    order = (2, 1, -1, 0)
    way = (1, -1, -1, 1)

    def at(d):
        return pl.ds(step(slow, d) * GROUP, GROUP)

    def block(d, n):
        return pl.ds(step(slow, d) * GROUP + step(fast, order[n]) * 2, 2)

    def slot(n):
        return pl.ds(2 * n, 2)

    def own_term(core, d, n):
        line_at, half = step(slow, d), n % 2
        y, x = (line_at, n // 2) if fast_is_x else (n // 2, line_at)
        return term((y * SIDE + x) * 2 + core, half)

    def fill(d):
        for n in range(GROUP):
            outgoing[step(slow, d) * GROUP + n] = own_term(1 - place.core, d, n)

    def merge(d):
        for n in range(GROUP):
            index = step(slow, d) * GROUP + n
            acc[index] = add(own_term(place.core, d, n), sib[index])

    for i, d in enumerate((2, 1, -1, 0)):
        fill(d)
        send(i, outgoing.at[at(d)], sib.at[at(d)], place.sibling())
        yield
    sent[0].wait_recv()
    merge(2)
    for n in range(4):
        send(4 + n, acc.at[block(2, n)], across.at[slot(n)], along_slow(way[n]))
    yield
    sent[1].wait_recv()
    merge(1)
    for n in (1, 2):
        send(8 + n, acc.at[block(1, n)], from_low.at[slot(n)], along_slow(1))
    yield
    sent[2].wait_recv()
    merge(-1)
    for n in (0, 3):
        send(8 + n, acc.at[block(-1, n)], from_high.at[slot(n)], along_slow(-1))
    yield
    sent[3].wait_recv()
    merge(0)
    yield
    for n in range(4):
        sent[4 + n].wait_recv()
        acc[block(way[n], n)] = add(acc[block(way[n], n)], across[slot(n)])
        target = from_low if way[n] == 1 else from_high
        send(12 + n, acc.at[block(way[n], n)], target.at[slot(n)], along_slow(way[n]))
        yield

    def settle(n):
        sent[8 + n].wait_recv()
        sent[12 + n].wait_recv()
        line[slot(n)] = add(acc[block(0, n)], from_low[slot(n)], from_high[slot(n)])

    settle(0)
    send(16, line.at[pl.ds(0, 1)], near_a, along_fast(1))
    send(17, line.at[pl.ds(1, 1)], near_b, along_fast(-1))
    yield
    settle(1)
    send(18, line.at[pl.ds(3, 1)], end_low.at[pl.ds(1, 1)], along_fast(1))
    yield
    settle(2)
    send(19, line.at[pl.ds(4, 1)], end_high.at[pl.ds(0, 1)], along_fast(-1))
    yield
    sent[16].wait_recv()
    line[pl.ds(2, 1)] = add(line[pl.ds(2, 1)], near_a[...])
    send(20, line.at[pl.ds(2, 1)], end_low.at[pl.ds(0, 1)], along_fast(1))
    yield
    sent[17].wait_recv()
    line[pl.ds(5, 1)] = add(line[pl.ds(5, 1)], near_b[...])
    send(21, line.at[pl.ds(5, 1)], end_high.at[pl.ds(1, 1)], along_fast(-1))
    yield
    settle(3)
    for i in (18, 19, 20, 21):
        sent[i].wait_recv()
    out[...] = add(line[slot(3)], end_low[...], end_high[...])
    for i in range(22):
        sent[i].wait_send()


SCATTER_BUFS = (SIDE * GROUP, SIDE * GROUP, SIDE * GROUP, GROUP, GROUP, GROUP, GROUP, 1, 1, 2, 2)


def dot(a, b, over):
    return lax.dot_general(a, b, ((over[:1], over[1:]), ((), ())), preferred_element_type=F32)


def attend_scatter_kernel(
    docs, pairs, q_ref, o_ref, g_ref, k_ref, v_ref, dq_ref, handed_ref, kg_ref, vg_ref,
    rank_of_pair, q_rows, g_rows, key_win, value_win, work, key_terms, value_terms, *scratch,
):
    count = len(SCATTER_BUFS)
    k_bufs, v_bufs = scratch[:count], scratch[count : 2 * count]
    k_send, k_recv, v_send, v_recv, hand_sem = scratch[2 * count :]
    place = Place()
    section, sections = lax.axis_index("pipe"), lax.axis_size("pipe")
    below = lax.rem(section + sections - 1, sections)
    above = lax.rem(section + 1, sections)
    barrier = pltpu.get_barrier_semaphore()
    for device in place.neighbours():
        pl.semaphore_signal(barrier, inc=1, device_id={"ctx": device}, device_id_type=MESH)
    for device in (below, above):
        pl.semaphore_signal(barrier, inc=1, device_id={"pipe": device}, device_id_type=MESH)
    scale = 1.0 / math.sqrt(HD)
    pair = pairs[lax.axis_index("ctx")]

    def note(p, carry):
        found = jnp.int32(0)
        for r in range(RANKS):
            found = jnp.maximum(found, jnp.where(pairs[r] == p, r, 0))
        rank_of_pair[p] = found
        return carry

    lax.fori_loop(0, RANKS, note, 0)

    def places(t):
        late = (t >= RANKS).astype(jnp.int32)
        rank = rank_of_pair[jnp.where(t >= RANKS, STRETCHES - 1 - t, t)]
        core, chip = lax.rem(rank, 2), rank // 2
        turned = lax.rem(chip, SIDE) * SIDE + chip // SIDE
        size = SIDE * SIDE
        return (core * size + chip) * 2 + late, (core * size + turned) * 2 + late

    for which in range(2):
        key_terms[which, WIN] = jnp.zeros((ST, HD), F32)
        value_terms[which, WIN] = jnp.zeros((ST, HD), F32)
    bases = (pair, STRETCHES - 1 - pair)
    lane = lax.rem(lax.broadcasted_iota(jnp.int32, (1, ROWS), 1), ST)
    for which in range(2):
        base = bases[which]
        lowest = (base - (WIN - 1)) * ST
        rows = slice(which * ST, (which + 1) * ST)
        for h in range(HQ):
            q_rows[h * ST : (h + 1) * ST] = q_ref[rows, h * HD : (h + 1) * HD]
            g_rows[h * ST : (h + 1) * ST] = g_ref[rows, h * HD : (h + 1) * HD]
        products = jnp.concatenate(
            [
                g_ref[rows, h * HD : (h + 1) * HD].astype(F32) * o_ref[rows, h * HD : (h + 1) * HD].astype(F32)
                for h in range(HQ)
            ],
            axis=0,
        )
        delta = jnp.sum(jnp.transpose(products), axis=0, keepdims=True)
        for j in range(WIN):
            k_at, v_at = places(jnp.maximum(base - (WIN - 1) + j, 0))
            key_win[j * ST : (j + 1) * ST] = k_ref[k_at]
            value_win[j * ST : (j + 1) * ST] = v_ref[v_at]
        position = base * ST + lane
        start, end = jnp.zeros_like(position), jnp.int32(0)
        for d in range(docs.shape[0]):
            end = end + docs[d]
            start = jnp.where(position >= end, end, start)
        low, high = start - lowest, position - lowest

        def scores(c, top):
            at = pl.multiple_of(c * CHUNK, CHUNK)
            found = dot(key_win[pl.ds(at, CHUNK)], q_rows[...], (1, 1))
            where = lax.broadcasted_iota(jnp.int32, (CHUNK, ROWS), 0) + at
            found = jnp.where((where >= low) & (where <= high), found, NEG)
            work[c] = found
            return jnp.maximum(top, jnp.max(found, axis=0, keepdims=True))

        top = lax.fori_loop(0, CHUNKS, scores, jnp.full((1, ROWS), NEG, F32))

        def weigh(c, total):
            weights = jnp.exp2((work[c] - top) * (scale * math.log2(math.e)))
            work[c] = weights
            return total + jnp.sum(weights, axis=0, keepdims=True)

        total = lax.fori_loop(0, CHUNKS, weigh, jnp.zeros((1, ROWS), F32))
        inverse = 1.0 / total

        def grads(c, dq_sum):
            at = pl.multiple_of(c * CHUNK, CHUNK)
            probs = work[c] * inverse
            value_terms[which, pl.ds(c * PART, PART)] = dot(probs.astype(BF16), g_rows[...], (1, 0)).reshape(PART, ST, HD)
            dprobs = dot(value_win[pl.ds(at, CHUNK)], g_rows[...], (1, 1))
            dscores = (probs * (dprobs - delta)).astype(BF16)
            key_terms[which, pl.ds(c * PART, PART)] = (dot(dscores, q_rows[...], (1, 0)) * scale).reshape(PART, ST, HD)
            turned = jnp.transpose(key_win[pl.ds(at, CHUNK)])
            return dq_sum + dot(turned, dscores, (1, 0))

        dq_sum = lax.fori_loop(0, CHUNKS, grads, jnp.zeros((HD, ROWS), F32))
        dq_rows = (jnp.transpose(dq_sum) * scale).astype(BF16)
        for h in range(HQ):
            dq_ref[rows, h * HD : (h + 1) * HD] = dq_rows[h * ST : (h + 1) * ST]

    early, late = bases[0] - (WIN - 1), bases[1] - (WIN - 1)

    def within(j):
        return jnp.where((j >= 0) & (j < WIN), j, WIN)

    def term_of(terms):
        def term(rank, half):
            t = pairs[rank] if half == 0 else STRETCHES - 1 - pairs[rank]
            return (terms[0, within(t - early)] + terms[1, within(t - late)]).astype(BF16)

        return term

    pl.semaphore_wait(barrier, 7)
    hand = pltpu.make_async_remote_copy(
        src_ref=dq_ref, dst_ref=handed_ref, send_sem=hand_sem.at[0], recv_sem=hand_sem.at[1],
        device_id={"pipe": below}, device_id_type=MESH,
    )
    hand.start()
    in_turn(
        scatter_stream(place, True, term_of(key_terms), kg_ref, k_bufs, k_send, k_recv),
        scatter_stream(place, False, term_of(value_terms), vg_ref, v_bufs, v_send, v_recv),
    )
    hand.wait()


def finish_kernel(*refs):
    for source, target in zip(refs[:4], refs[4:]):
        target[...] = source[...]


def on_device(queries, keys, values, attn_out, grad_out, doc_lengths, pair_of_rank):
    vmem = pl.BlockSpec(memory_space=pltpu.VMEM)
    smem = pl.BlockSpec(memory_space=pltpu.SMEM)
    hbm = pl.BlockSpec(memory_space=pl.ANY)
    full = jax.ShapeDtypeStruct((STRETCHES, ST, HD), BF16)
    own = jax.ShapeDtypeStruct((2, ST, HD), BF16)
    tok = 2 * ST
    dma = pltpu.SemaphoreType.DMA
    all_keys, all_values = pl.pallas_call(
        gather_kernel,
        out_shape=(full, full),
        in_specs=[vmem] * 2,
        out_specs=(vmem, vmem),
        scratch_shapes=[dma((2,))] + [dma((23,))] * 4,
        compiler_params=pltpu.CompilerParams(collective_id=0, has_side_effects=True),
        name="gather_keys_values",
    )(keys.reshape(2, ST, HD), values.reshape(2, ST, HD))
    bufs = [pltpu.VMEM((n, ST, HD), BF16) for n in SCATTER_BUFS]
    wide = jax.ShapeDtypeStruct((tok, HQ * HD), BF16)
    results = pl.pallas_call(
        attend_scatter_kernel,
        out_shape=(wide, wide, own, own),
        in_specs=[smem] * 2 + [vmem] * 5,
        out_specs=(vmem, hbm, vmem, vmem),
        scratch_shapes=[
            pltpu.SMEM((RANKS,), jnp.int32),
            pltpu.VMEM((ROWS, HD), BF16),
            pltpu.VMEM((ROWS, HD), BF16),
            pltpu.VMEM((WIN * ST, HD), BF16),
            pltpu.VMEM((WIN * ST, HD), BF16),
            pltpu.VMEM((CHUNKS, CHUNK, ROWS), F32),
            pltpu.VMEM((2, WIN + 1, ST, HD), F32),
            pltpu.VMEM((2, WIN + 1, ST, HD), F32),
        ]
        + bufs
        + bufs
        + [dma((22,))] * 4
        + [dma((2,))],
        compiler_params=pltpu.CompilerParams(collective_id=1, has_side_effects=True),
        name="attend_scatter",
    )(doc_lengths, pair_of_rank, queries[0], attn_out[0], grad_out[0], all_keys, all_values)
    query_grad, handed, key_grad, value_grad = pl.pallas_call(
        finish_kernel,
        out_shape=(wide, wide, own, own),
        in_specs=[vmem] * 4,
        out_specs=(vmem,) * 4,
        name="finish",
    )(*results)
    return (
        query_grad[None],
        handed[None],
        key_grad.reshape(1, tok, HD),
        value_grad.reshape(1, tok, HD),
    )


def solution(mesh):
    split = P("pipe", "ctx", None)
    return jax.shard_map(
        on_device,
        mesh=mesh,
        in_specs=(split,) * 5 + (P(), P()),
        out_specs=(split,) * 4,
        check_vma=False,
    )
```

```python
import math

import jax
import jax.numpy as jnp
from jax import lax
from jax.experimental import pallas as pl
from jax.experimental.pallas import tpu as pltpu
from jax.sharding import PartitionSpec as P

HQ = 8
HD = 128
ST = 64
RANKS = 32
SIDE = 4
STRETCHES = 2 * RANKS
WIN = 18
CHUNK = 384
PART = CHUNK // ST
CHUNKS = WIN * ST // CHUNK
ROWS = HQ * ST
GROUP = 2 * SIDE
NEG = -1e30
MESH = pl.DeviceIdType.MESH
F32 = jnp.float32
BF16 = jnp.bfloat16


class Place:
    def __init__(self):
        me = lax.axis_index("ctx")
        self.core = lax.rem(me, 2)
        chip = me // 2
        self.x = lax.rem(chip, SIDE)
        self.y = chip // SIDE

    def at(self, dx, dy):
        x = lax.rem(self.x + dx + SIDE, SIDE)
        y = lax.rem(self.y + dy + SIDE, SIDE)
        return (y * SIDE + x) * 2 + self.core

    def sibling(self):
        return (self.y * SIDE + self.x) * 2 + 1 - self.core

    def neighbours(self):
        steps = [(1, 0), (-1, 0), (2, 0), (0, 1), (0, -1), (0, 2)]
        return [self.sibling()] + [self.at(dx, dy) for dx, dy in steps]

    def order(self, fast_is_x):
        if fast_is_x:
            return self.x, self.y, (lambda d: self.at(d, 0)), (lambda d: self.at(0, d))
        return self.y, self.x, (lambda d: self.at(0, d)), (lambda d: self.at(d, 0))


def step(i, d):
    return lax.rem(i + d + SIDE, SIDE)


def in_turn(*streams):
    live = list(streams)
    while live:
        for stream in list(live):
            if next(stream, StopIteration) is StopIteration:
                live.remove(stream)


def sender(send_sem, recv_sem):
    sent = {}

    def send(i, src, dst, device):
        copy = pltpu.make_async_remote_copy(
            src_ref=src, dst_ref=dst, send_sem=send_sem.at[i], recv_sem=recv_sem.at[i],
            device_id={"ctx": device}, device_id_type=MESH,
        )
        copy.start()
        sent[i] = copy

    return sent, send


def gather_stream(place, fast_is_x, own, full, own_sem, send_sem, recv_sem):
    fast, slow, along_fast, along_slow = place.order(fast_is_x)
    sent, send = sender(send_sem, recv_sem)
    half = place.core * (SIDE * GROUP)

    def block(f, d=0):
        return full.at[pl.ds(half + step(slow, d) * GROUP + step(fast, f) * 2, 2)]

    def group(d):
        return full.at[pl.ds(half + step(slow, d) * GROUP, GROUP)]

    def spread(i, f, src=None):
        src = block(f) if src is None else src
        send(i, src, block(f), along_slow(1))
        send(i + 1, src, block(f), along_slow(-1))

    def relay(i, f, toward):
        send(i, block(f, -toward), block(f, -toward), along_slow(toward))

    send(0, own, block(0), along_fast(1))
    send(1, own, block(0), along_fast(-1))
    send(2, own, block(0), along_fast(2))
    spread(4, 0, own)
    mine = pltpu.make_async_copy(own, block(0), own_sem)
    mine.start()
    yield
    sent[0].wait_recv()
    spread(6, -1)
    yield
    sent[1].wait_recv()
    spread(8, 1)
    yield
    sent[4].wait_recv()
    relay(12, 0, 1)
    yield
    sent[2].wait_recv()
    spread(10, 2)
    send(15, block(2), block(2), along_slow(2))
    mine.wait()
    send(16, group(0), group(0), place.sibling())
    yield
    sent[7].wait_recv()
    relay(13, -1, -1)
    yield
    sent[9].wait_recv()
    relay(14, 1, -1)
    yield
    sent[6].wait_recv()
    sent[8].wait_recv()
    sent[10].wait_recv()
    send(17, group(-1), group(-1), place.sibling())
    yield
    sent[5].wait_recv()
    sent[11].wait_recv()
    send(18, group(1), group(1), place.sibling())
    yield
    for n, f in enumerate((0, -1, 1, 2)):
        sent[12 + n].wait_recv()
        send(19 + n, block(f, 2), block(f, 2), place.sibling())
        yield
    for i in range(16, 23):
        sent[i].wait_recv()
    for copy in sent.values():
        copy.wait_send()


def gather_kernel(k_ref, v_ref, gk_ref, gv_ref, own_sem, k_send, k_recv, v_send, v_recv):
    place = Place()
    barrier = pltpu.get_barrier_semaphore()
    for device in place.neighbours():
        pl.semaphore_signal(barrier, inc=1, device_id={"ctx": device}, device_id_type=MESH)
    pl.semaphore_wait(barrier, 7)
    in_turn(
        gather_stream(place, True, k_ref, gk_ref, own_sem.at[0], k_send, k_recv),
        gather_stream(place, False, v_ref, gv_ref, own_sem.at[1], v_send, v_recv),
    )


def add(*terms):
    total = terms[0].astype(F32)
    for term in terms[1:]:
        total = total + term.astype(F32)
    return total.astype(BF16)


def scatter_stream(place, fast_is_x, term, out, bufs, send_sem, recv_sem):
    outgoing, sib, acc, across, from_low, from_high, line, far, end_low, end_high = bufs
    fast, slow, along_fast, along_slow = place.order(fast_is_x)
    sent, send = sender(send_sem, recv_sem)
    order = (2, 1, -1, 0)
    way = (1, -1, -1, 1)

    def at(d):
        return pl.ds(step(slow, d) * GROUP, GROUP)

    def block(d, n):
        return pl.ds(step(slow, d) * GROUP + step(fast, order[n]) * 2, 2)

    def slot(n):
        return pl.ds(2 * n, 2)

    def own_term(core, d, n):
        line_at, half = step(slow, d), n % 2
        y, x = (line_at, n // 2) if fast_is_x else (n // 2, line_at)
        return term((y * SIDE + x) * 2 + core, half)

    def fill(d):
        for n in range(GROUP):
            outgoing[step(slow, d) * GROUP + n] = own_term(1 - place.core, d, n)

    def merge(d):
        for n in range(GROUP):
            index = step(slow, d) * GROUP + n
            acc[index] = add(own_term(place.core, d, n), sib[index])

    for i, d in enumerate((2, 1, -1, 0)):
        fill(d)
        send(i, outgoing.at[at(d)], sib.at[at(d)], place.sibling())
        yield
    sent[0].wait_recv()
    merge(2)
    for n in range(4):
        send(4 + n, acc.at[block(2, n)], across.at[slot(n)], along_slow(way[n]))
    yield
    sent[1].wait_recv()
    merge(1)
    for n in (1, 2):
        send(8 + n, acc.at[block(1, n)], from_low.at[slot(n)], along_slow(1))
    yield
    sent[2].wait_recv()
    merge(-1)
    for n in (0, 3):
        send(8 + n, acc.at[block(-1, n)], from_high.at[slot(n)], along_slow(-1))
    yield
    sent[3].wait_recv()
    merge(0)
    yield
    for n in range(4):
        sent[4 + n].wait_recv()
        acc[block(way[n], n)] = add(acc[block(way[n], n)], across[slot(n)])
        target = from_low if way[n] == 1 else from_high
        send(12 + n, acc.at[block(way[n], n)], target.at[slot(n)], along_slow(way[n]))
        yield

    def settle(n):
        sent[8 + n].wait_recv()
        sent[12 + n].wait_recv()
        line[slot(n)] = add(acc[block(0, n)], from_low[slot(n)], from_high[slot(n)])

    settle(0)
    send(16, line.at[slot(0)], far, along_fast(2))
    yield
    settle(1)
    send(17, line.at[slot(1)], end_low, along_fast(1))
    yield
    settle(2)
    send(18, line.at[slot(2)], end_high, along_fast(-1))
    yield
    settle(3)
    for i in (16, 17, 18):
        sent[i].wait_recv()
    out[...] = add(line[slot(3)], end_low[...], end_high[...], far[...])
    for copy in sent.values():
        copy.wait_send()


SCATTER_BUFS = (SIDE * GROUP, SIDE * GROUP, SIDE * GROUP, GROUP, GROUP, GROUP, GROUP, 2, 2, 2)


def dot(a, b, over):
    return lax.dot_general(a, b, ((over[:1], over[1:]), ((), ())), preferred_element_type=F32)


def attend_scatter_kernel(
    docs, pairs, q_ref, o_ref, g_ref, k_ref, v_ref, dq_ref, handed_ref, kg_ref, vg_ref,
    rank_of_pair, q_rows, g_rows, key_win, value_win, work, key_terms, value_terms, *scratch,
):
    count = len(SCATTER_BUFS)
    k_bufs, v_bufs = scratch[:count], scratch[count : 2 * count]
    k_send, k_recv, v_send, v_recv, hand_sem = scratch[2 * count :]
    place = Place()
    section, sections = lax.axis_index("pipe"), lax.axis_size("pipe")
    below = lax.rem(section + sections - 1, sections)
    above = lax.rem(section + 1, sections)
    barrier = pltpu.get_barrier_semaphore()
    for device in place.neighbours():
        pl.semaphore_signal(barrier, inc=1, device_id={"ctx": device}, device_id_type=MESH)
    for device in (below, above):
        pl.semaphore_signal(barrier, inc=1, device_id={"pipe": device}, device_id_type=MESH)
    scale = 1.0 / math.sqrt(HD)
    pair = pairs[lax.axis_index("ctx")]

    def note(p, carry):
        found = jnp.int32(0)
        for r in range(RANKS):
            found = jnp.maximum(found, jnp.where(pairs[r] == p, r, 0))
        rank_of_pair[p] = found
        return carry

    lax.fori_loop(0, RANKS, note, 0)

    def places(t):
        late = (t >= RANKS).astype(jnp.int32)
        rank = rank_of_pair[jnp.where(t >= RANKS, STRETCHES - 1 - t, t)]
        core, chip = lax.rem(rank, 2), rank // 2
        turned = lax.rem(chip, SIDE) * SIDE + chip // SIDE
        size = SIDE * SIDE
        return (core * size + chip) * 2 + late, (core * size + turned) * 2 + late

    for which in range(2):
        key_terms[which, WIN] = jnp.zeros((ST, HD), F32)
        value_terms[which, WIN] = jnp.zeros((ST, HD), F32)
    bases = (pair, STRETCHES - 1 - pair)
    lane = lax.rem(lax.broadcasted_iota(jnp.int32, (1, ROWS), 1), ST)
    for which in range(2):
        base = bases[which]
        lowest = (base - (WIN - 1)) * ST
        rows = slice(which * ST, (which + 1) * ST)
        for h in range(HQ):
            q_rows[h * ST : (h + 1) * ST] = q_ref[rows, h * HD : (h + 1) * HD]
            g_rows[h * ST : (h + 1) * ST] = g_ref[rows, h * HD : (h + 1) * HD]
        products = jnp.concatenate(
            [
                g_ref[rows, h * HD : (h + 1) * HD].astype(F32) * o_ref[rows, h * HD : (h + 1) * HD].astype(F32)
                for h in range(HQ)
            ],
            axis=0,
        )
        delta = jnp.sum(jnp.transpose(products), axis=0, keepdims=True)
        for j in range(WIN):
            k_at, v_at = places(jnp.maximum(base - (WIN - 1) + j, 0))
            key_win[j * ST : (j + 1) * ST] = k_ref[k_at]
            value_win[j * ST : (j + 1) * ST] = v_ref[v_at]
        position = base * ST + lane
        start, end = jnp.zeros_like(position), jnp.int32(0)
        for d in range(docs.shape[0]):
            end = end + docs[d]
            start = jnp.where(position >= end, end, start)
        low, high = start - lowest, position - lowest

        def scores(c, top):
            at = pl.multiple_of(c * CHUNK, CHUNK)
            found = dot(key_win[pl.ds(at, CHUNK)], q_rows[...], (1, 1))
            where = lax.broadcasted_iota(jnp.int32, (CHUNK, ROWS), 0) + at
            found = jnp.where((where >= low) & (where <= high), found, NEG)
            work[c] = found
            return jnp.maximum(top, jnp.max(found, axis=0, keepdims=True))

        top = lax.fori_loop(0, CHUNKS, scores, jnp.full((1, ROWS), NEG, F32))

        def weigh(c, total):
            weights = jnp.exp2((work[c] - top) * (scale * math.log2(math.e)))
            work[c] = weights
            return total + jnp.sum(weights, axis=0, keepdims=True)

        total = lax.fori_loop(0, CHUNKS, weigh, jnp.zeros((1, ROWS), F32))
        inverse = 1.0 / total

        def grads(c, dq_sum):
            at = pl.multiple_of(c * CHUNK, CHUNK)
            probs = work[c] * inverse
            value_terms[which, pl.ds(c * PART, PART)] = dot(probs.astype(BF16), g_rows[...], (1, 0)).reshape(PART, ST, HD)
            dprobs = dot(value_win[pl.ds(at, CHUNK)], g_rows[...], (1, 1))
            dscores = (probs * (dprobs - delta)).astype(BF16)
            key_terms[which, pl.ds(c * PART, PART)] = (dot(dscores, q_rows[...], (1, 0)) * scale).reshape(PART, ST, HD)
            turned = jnp.transpose(key_win[pl.ds(at, CHUNK)])
            return dq_sum + dot(turned, dscores, (1, 0))

        dq_sum = lax.fori_loop(0, CHUNKS, grads, jnp.zeros((HD, ROWS), F32))
        dq_rows = (jnp.transpose(dq_sum) * scale).astype(BF16)
        for h in range(HQ):
            dq_ref[rows, h * HD : (h + 1) * HD] = dq_rows[h * ST : (h + 1) * ST]

    early, late = bases[0] - (WIN - 1), bases[1] - (WIN - 1)

    def within(j):
        return jnp.where((j >= 0) & (j < WIN), j, WIN)

    def term_of(terms):
        def term(rank, half):
            t = pairs[rank] if half == 0 else STRETCHES - 1 - pairs[rank]
            return (terms[0, within(t - early)] + terms[1, within(t - late)]).astype(BF16)

        return term

    pl.semaphore_wait(barrier, 9)
    hand = pltpu.make_async_remote_copy(
        src_ref=dq_ref, dst_ref=handed_ref, send_sem=hand_sem.at[0], recv_sem=hand_sem.at[1],
        device_id={"pipe": below}, device_id_type=MESH,
    )
    hand.start()
    in_turn(
        scatter_stream(place, True, term_of(key_terms), kg_ref, k_bufs, k_send, k_recv),
        scatter_stream(place, False, term_of(value_terms), vg_ref, v_bufs, v_send, v_recv),
    )
    hand.wait()


def finish_kernel(*refs):
    for source, target in zip(refs[:4], refs[4:]):
        target[...] = source[...]


def on_device(queries, keys, values, attn_out, grad_out, doc_lengths, pair_of_rank):
    vmem = pl.BlockSpec(memory_space=pltpu.VMEM)
    smem = pl.BlockSpec(memory_space=pltpu.SMEM)
    hbm = pl.BlockSpec(memory_space=pl.ANY)
    full = jax.ShapeDtypeStruct((STRETCHES, ST, HD), BF16)
    own = jax.ShapeDtypeStruct((2, ST, HD), BF16)
    tok = 2 * ST
    dma = pltpu.SemaphoreType.DMA
    all_keys, all_values = pl.pallas_call(
        gather_kernel,
        out_shape=(full, full),
        in_specs=[vmem] * 2,
        out_specs=(vmem, vmem),
        scratch_shapes=[dma((2,))] + [dma((23,))] * 4,
        compiler_params=pltpu.CompilerParams(collective_id=0, has_side_effects=True, vmem_limit_bytes=8 << 20),
        cost_estimate=pl.CostEstimate(flops=2**33, bytes_accessed=2**26, transcendentals=0),
        name="gather_keys_values",
    )(keys.reshape(2, ST, HD), values.reshape(2, ST, HD))
    bufs = [pltpu.VMEM((n, ST, HD), BF16) for n in SCATTER_BUFS]
    wide = jax.ShapeDtypeStruct((tok, HQ * HD), BF16)
    results = pl.pallas_call(
        attend_scatter_kernel,
        out_shape=(wide, wide, own, own),
        in_specs=[smem] * 2 + [vmem] * 5,
        out_specs=(vmem, hbm, vmem, vmem),
        scratch_shapes=[
            pltpu.SMEM((RANKS,), jnp.int32),
            pltpu.VMEM((ROWS, HD), BF16),
            pltpu.VMEM((ROWS, HD), BF16),
            pltpu.VMEM((WIN * ST, HD), BF16),
            pltpu.VMEM((WIN * ST, HD), BF16),
            pltpu.VMEM((CHUNKS, CHUNK, ROWS), F32),
            pltpu.VMEM((2, WIN + 1, ST, HD), F32),
            pltpu.VMEM((2, WIN + 1, ST, HD), F32),
        ]
        + bufs
        + bufs
        + [dma((19,))] * 4
        + [dma((2,))],
        compiler_params=pltpu.CompilerParams(collective_id=1, has_side_effects=True, vmem_limit_bytes=28 << 20),
        cost_estimate=pl.CostEstimate(flops=2**33, bytes_accessed=2**26, transcendentals=0),
        name="attend_scatter",
    )(doc_lengths, pair_of_rank, queries[0], attn_out[0], grad_out[0], all_keys, all_values)
    query_grad, handed, key_grad, value_grad = pl.pallas_call(
        finish_kernel,
        out_shape=(wide, wide, own, own),
        in_specs=[vmem] * 4,
        out_specs=(vmem,) * 4,
        compiler_params=pltpu.CompilerParams(vmem_limit_bytes=4 << 20),
        name="finish",
    )(*results)
    return (
        query_grad[None],
        handed[None],
        key_grad.reshape(1, tok, HD),
        value_grad.reshape(1, tok, HD),
    )


def solution(mesh):
    split = P("pipe", "ctx", None)
    return jax.shard_map(
        on_device,
        mesh=mesh,
        in_specs=(split,) * 5 + (P(), P()),
        out_specs=(split,) * 4,
        check_vma=False,
    )
```

```python
import math

import jax
import jax.numpy as jnp
from jax import lax
from jax.experimental import pallas as pl
from jax.experimental.pallas import tpu as pltpu
from jax.sharding import PartitionSpec as P

HQ = 8
HD = 128
ST = 64
RANKS = 32
SIDE = 4
STRETCHES = 2 * RANKS
WIN = 18
CHUNK = 384
PART = CHUNK // ST
CHUNKS = WIN * ST // CHUNK
ROWS = HQ * ST
GROUP = 2 * SIDE
NEG = -1e30
MESH = pl.DeviceIdType.MESH
F32 = jnp.float32
BF16 = jnp.bfloat16


class Place:
    def __init__(self):
        me = lax.axis_index("ctx")
        self.core = lax.rem(me, 2)
        chip = me // 2
        self.x = lax.rem(chip, SIDE)
        self.y = chip // SIDE

    def at(self, dx, dy):
        x = lax.rem(self.x + dx + SIDE, SIDE)
        y = lax.rem(self.y + dy + SIDE, SIDE)
        return (y * SIDE + x) * 2 + self.core

    def sibling(self):
        return (self.y * SIDE + self.x) * 2 + 1 - self.core

    def neighbours(self):
        steps = [(1, 0), (-1, 0), (2, 0), (0, 1), (0, -1), (0, 2)]
        return [self.sibling()] + [self.at(dx, dy) for dx, dy in steps]

    def order(self, fast_is_x):
        if fast_is_x:
            return self.x, self.y, (lambda d: self.at(d, 0)), (lambda d: self.at(0, d))
        return self.y, self.x, (lambda d: self.at(0, d)), (lambda d: self.at(d, 0))


def step(i, d):
    return lax.rem(i + d + SIDE, SIDE)


def in_turn(*streams):
    live = list(streams)
    while live:
        for stream in list(live):
            if next(stream, StopIteration) is StopIteration:
                live.remove(stream)


def sender(send_sem, recv_sem):
    sent = {}

    def send(i, src, dst, device):
        copy = pltpu.make_async_remote_copy(
            src_ref=src, dst_ref=dst, send_sem=send_sem.at[i], recv_sem=recv_sem.at[i],
            device_id={"ctx": device}, device_id_type=MESH,
        )
        copy.start()
        sent[i] = copy

    return sent, send


def gather_stream(place, fast_is_x, own, full, own_sem, send_sem, recv_sem):
    fast, slow, along_fast, along_slow = place.order(fast_is_x)
    sent, send = sender(send_sem, recv_sem)
    half = place.core * (SIDE * GROUP)

    def block(f, d=0):
        return full.at[pl.ds(half + step(slow, d) * GROUP + step(fast, f) * 2, 2)]

    def group(d):
        return full.at[pl.ds(half + step(slow, d) * GROUP, GROUP)]

    def spread(i, f, src=None):
        src = block(f) if src is None else src
        send(i, src, block(f), along_slow(1))
        send(i + 1, src, block(f), along_slow(-1))

    def relay(i, f, toward):
        send(i, block(f, -toward), block(f, -toward), along_slow(toward))

    send(0, own, block(0), along_fast(1))
    send(1, own, block(0), along_fast(-1))
    send(2, own, block(0), along_fast(2))
    spread(4, 0, own)
    mine = pltpu.make_async_copy(own, block(0), own_sem)
    mine.start()
    yield
    sent[0].wait_recv()
    spread(6, -1)
    yield
    sent[1].wait_recv()
    spread(8, 1)
    yield
    sent[4].wait_recv()
    relay(12, 0, 1)
    yield
    sent[2].wait_recv()
    spread(10, 2)
    send(15, block(2), block(2), along_slow(2))
    mine.wait()
    send(16, group(0), group(0), place.sibling())
    yield
    sent[7].wait_recv()
    relay(13, -1, -1)
    yield
    sent[9].wait_recv()
    relay(14, 1, -1)
    yield
    sent[6].wait_recv()
    sent[8].wait_recv()
    sent[10].wait_recv()
    send(17, group(-1), group(-1), place.sibling())
    yield
    sent[5].wait_recv()
    sent[11].wait_recv()
    send(18, group(1), group(1), place.sibling())
    yield
    for n, f in enumerate((0, -1, 1, 2)):
        sent[12 + n].wait_recv()
        send(19 + n, block(f, 2), block(f, 2), place.sibling())
        yield
    for i in range(16, 23):
        sent[i].wait_recv()
    for copy in sent.values():
        copy.wait_send()


def gather_kernel(k_ref, v_ref, gk_ref, gv_ref, own_sem, k_send, k_recv, v_send, v_recv):
    place = Place()
    barrier = pltpu.get_barrier_semaphore()
    for device in place.neighbours():
        pl.semaphore_signal(barrier, inc=1, device_id={"ctx": device}, device_id_type=MESH)
    pl.semaphore_wait(barrier, 7)
    in_turn(
        gather_stream(place, True, k_ref, gk_ref, own_sem.at[0], k_send, k_recv),
        gather_stream(place, False, v_ref, gv_ref, own_sem.at[1], v_send, v_recv),
    )


def add(*terms):
    total = terms[0].astype(F32)
    for term in terms[1:]:
        total = total + term.astype(F32)
    return total.astype(BF16)


def scatter_stream(place, fast_is_x, term, out, bufs, send_sem, recv_sem):
    outgoing, sib, acc, across, from_low, from_high, line, far, end_low, end_high = bufs
    fast, slow, along_fast, along_slow = place.order(fast_is_x)
    sent, send = sender(send_sem, recv_sem)
    order = (2, 1, -1, 0)
    way = (1, -1, -1, 1)

    def at(d):
        return pl.ds(step(slow, d) * GROUP, GROUP)

    def block(d, n):
        return pl.ds(step(slow, d) * GROUP + step(fast, order[n]) * 2, 2)

    def slot(n):
        return pl.ds(2 * n, 2)

    def own_term(core, d, n):
        line_at, half = step(slow, d), n % 2
        y, x = (line_at, n // 2) if fast_is_x else (n // 2, line_at)
        return term((y * SIDE + x) * 2 + core, half)

    def own_terms(core, d):
        return jnp.stack([own_term(core, d, n) for n in range(GROUP)])

    def prepare(d):
        acc[at(d)] = own_terms(place.core, d)

    def merge(d):
        acc[at(d)] = add(acc[at(d)], sib[at(d)])

    for i, d in enumerate((2, 1, -1, 0)):
        outgoing[at(d)] = own_terms(1 - place.core, d)
        send(i, outgoing.at[at(d)], sib.at[at(d)], place.sibling())
        yield
    prepare(2)
    yield
    sent[0].wait_recv()
    merge(2)
    for n in range(4):
        send(4 + n, acc.at[block(2, n)], across.at[slot(n)], along_slow(way[n]))
    prepare(1)
    yield
    sent[1].wait_recv()
    merge(1)
    for n in (1, 2):
        send(8 + n, acc.at[block(1, n)], from_low.at[slot(n)], along_slow(1))
    prepare(-1)
    yield
    sent[2].wait_recv()
    merge(-1)
    for n in (0, 3):
        send(8 + n, acc.at[block(-1, n)], from_high.at[slot(n)], along_slow(-1))
    prepare(0)
    yield
    sent[3].wait_recv()
    merge(0)
    yield
    for n in range(4):
        sent[4 + n].wait_recv()
        acc[block(way[n], n)] = add(acc[block(way[n], n)], across[slot(n)])
        target = from_low if way[n] == 1 else from_high
        send(12 + n, acc.at[block(way[n], n)], target.at[slot(n)], along_slow(way[n]))
        yield

    def settle(n):
        sent[8 + n].wait_recv()
        sent[12 + n].wait_recv()
        line[slot(n)] = add(acc[block(0, n)], from_low[slot(n)], from_high[slot(n)])

    settle(0)
    send(16, line.at[slot(0)], far, along_fast(2))
    yield
    settle(1)
    send(17, line.at[slot(1)], end_low, along_fast(1))
    yield
    settle(2)
    send(18, line.at[slot(2)], end_high, along_fast(-1))
    yield
    settle(3)
    for i in (16, 17, 18):
        sent[i].wait_recv()
    out[...] = add(line[slot(3)], end_low[...], end_high[...], far[...])
    for copy in sent.values():
        copy.wait_send()


SCATTER_BUFS = (SIDE * GROUP, SIDE * GROUP, SIDE * GROUP, GROUP, GROUP, GROUP, GROUP, 2, 2, 2)


def dot(a, b, over):
    return lax.dot_general(a, b, ((over[:1], over[1:]), ((), ())), preferred_element_type=F32)


def attend_scatter_kernel(
    docs, pairs, q_ref, o_ref, g_ref, k_ref, v_ref, dq_ref, handed_ref, kg_ref, vg_ref,
    rank_of_pair, q_rows, g_rows, key_win, value_win, work, key_terms, value_terms, *scratch,
):
    count = len(SCATTER_BUFS)
    k_bufs, v_bufs = scratch[:count], scratch[count : 2 * count]
    k_send, k_recv, v_send, v_recv, hand_sem = scratch[2 * count :]
    place = Place()
    section, sections = lax.axis_index("pipe"), lax.axis_size("pipe")
    below = lax.rem(section + sections - 1, sections)
    above = lax.rem(section + 1, sections)
    barrier = pltpu.get_barrier_semaphore()
    for device in place.neighbours():
        pl.semaphore_signal(barrier, inc=1, device_id={"ctx": device}, device_id_type=MESH)
    for device in (below, above):
        pl.semaphore_signal(barrier, inc=1, device_id={"pipe": device}, device_id_type=MESH)
    scale = 1.0 / math.sqrt(HD)
    pair = pairs[lax.axis_index("ctx")]

    def note(p, carry):
        found = jnp.int32(0)
        for r in range(RANKS):
            found = jnp.maximum(found, jnp.where(pairs[r] == p, r, 0))
        rank_of_pair[p] = found
        return carry

    lax.fori_loop(0, RANKS, note, 0)

    def places(t):
        late = (t >= RANKS).astype(jnp.int32)
        rank = rank_of_pair[jnp.where(t >= RANKS, STRETCHES - 1 - t, t)]
        core, chip = lax.rem(rank, 2), rank // 2
        turned = lax.rem(chip, SIDE) * SIDE + chip // SIDE
        size = SIDE * SIDE
        return (core * size + chip) * 2 + late, (core * size + turned) * 2 + late

    for which in range(2):
        key_terms[which, WIN] = jnp.zeros((ST, HD), F32)
        value_terms[which, WIN] = jnp.zeros((ST, HD), F32)
    bases = (pair, STRETCHES - 1 - pair)
    lane = lax.rem(lax.broadcasted_iota(jnp.int32, (1, ROWS), 1), ST)
    for which in range(2):
        base = bases[which]
        lowest = (base - (WIN - 1)) * ST
        rows = slice(which * ST, (which + 1) * ST)
        for h in range(HQ):
            q_rows[h * ST : (h + 1) * ST] = q_ref[rows, h * HD : (h + 1) * HD]
            g_rows[h * ST : (h + 1) * ST] = g_ref[rows, h * HD : (h + 1) * HD]
        products = jnp.concatenate(
            [
                g_ref[rows, h * HD : (h + 1) * HD].astype(F32) * o_ref[rows, h * HD : (h + 1) * HD].astype(F32)
                for h in range(HQ)
            ],
            axis=0,
        )
        delta = jnp.sum(jnp.transpose(products), axis=0, keepdims=True)
        for j in range(WIN):
            k_at, v_at = places(jnp.maximum(base - (WIN - 1) + j, 0))
            key_win[j * ST : (j + 1) * ST] = k_ref[k_at]
            value_win[j * ST : (j + 1) * ST] = v_ref[v_at]
        position = base * ST + lane
        start, end = jnp.zeros_like(position), jnp.int32(0)
        for d in range(docs.shape[0]):
            end = end + docs[d]
            start = jnp.where(position >= end, end, start)
        low, high = start - lowest, position - lowest

        def scores(c, top):
            at = pl.multiple_of(c * CHUNK, CHUNK)
            found = dot(key_win[pl.ds(at, CHUNK)], q_rows[...], (1, 1))
            where = lax.broadcasted_iota(jnp.int32, (CHUNK, ROWS), 0) + at
            found = jnp.where((where >= low) & (where <= high), found, NEG)
            work[c] = found
            return jnp.maximum(top, jnp.max(found, axis=0, keepdims=True))

        top = lax.fori_loop(0, CHUNKS, scores, jnp.full((1, ROWS), NEG, F32))

        def weigh(c, total):
            weights = jnp.exp2((work[c] - top) * (scale * math.log2(math.e)))
            work[c] = weights
            return total + jnp.sum(weights, axis=0, keepdims=True)

        total = lax.fori_loop(0, CHUNKS, weigh, jnp.zeros((1, ROWS), F32))
        inverse = 1.0 / total

        def grads(c, dq_sum):
            at = pl.multiple_of(c * CHUNK, CHUNK)
            probs = work[c] * inverse
            value_terms[which, pl.ds(c * PART, PART)] = dot(probs.astype(BF16), g_rows[...], (1, 0)).reshape(PART, ST, HD)
            dprobs = dot(value_win[pl.ds(at, CHUNK)], g_rows[...], (1, 1))
            dscores = (probs * (dprobs - delta)).astype(BF16)
            key_terms[which, pl.ds(c * PART, PART)] = (dot(dscores, q_rows[...], (1, 0)) * scale).reshape(PART, ST, HD)
            turned = jnp.transpose(key_win[pl.ds(at, CHUNK)])
            return dq_sum + dot(turned, dscores, (1, 0))

        dq_sum = lax.fori_loop(0, CHUNKS, grads, jnp.zeros((HD, ROWS), F32))
        dq_rows = (jnp.transpose(dq_sum) * scale).astype(BF16)
        for h in range(HQ):
            dq_ref[rows, h * HD : (h + 1) * HD] = dq_rows[h * ST : (h + 1) * ST]

    early, late = bases[0] - (WIN - 1), bases[1] - (WIN - 1)

    def within(j):
        return jnp.where((j >= 0) & (j < WIN), j, WIN)

    def term_of(terms):
        def term(rank, half):
            t = pairs[rank] if half == 0 else STRETCHES - 1 - pairs[rank]
            return (terms[0, within(t - early)] + terms[1, within(t - late)]).astype(BF16)

        return term

    pl.semaphore_wait(barrier, 9)
    hand = pltpu.make_async_remote_copy(
        src_ref=dq_ref, dst_ref=handed_ref, send_sem=hand_sem.at[0], recv_sem=hand_sem.at[1],
        device_id={"pipe": below}, device_id_type=MESH,
    )
    hand.start()
    in_turn(
        scatter_stream(place, True, term_of(key_terms), kg_ref, k_bufs, k_send, k_recv),
        scatter_stream(place, False, term_of(value_terms), vg_ref, v_bufs, v_send, v_recv),
    )
    hand.wait()


def finish_kernel(*refs):
    for source, target in zip(refs[:4], refs[4:]):
        target[...] = source[...]


def in_hbm(x):
    return pltpu.with_memory_space_constraint(x, pltpu.HBM)


def on_device(queries, keys, values, attn_out, grad_out, doc_lengths, pair_of_rank):
    vmem = pl.BlockSpec(memory_space=pltpu.VMEM)
    smem = pl.BlockSpec(memory_space=pltpu.SMEM)
    hbm = pl.BlockSpec(memory_space=pl.ANY)
    full = jax.ShapeDtypeStruct((STRETCHES, ST, HD), BF16)
    own = jax.ShapeDtypeStruct((2, ST, HD), BF16)
    tok = 2 * ST
    dma = pltpu.SemaphoreType.DMA
    all_keys, all_values = pl.pallas_call(
        gather_kernel,
        out_shape=(full, full),
        in_specs=[pl.BlockSpec(memory_space=pltpu.HBM)] * 2,
        out_specs=(vmem, vmem),
        scratch_shapes=[dma((2,))] + [dma((23,))] * 4,
        compiler_params=pltpu.CompilerParams(collective_id=0, has_side_effects=True, vmem_limit_bytes=8 << 20),
        cost_estimate=pl.CostEstimate(flops=2**33, bytes_accessed=2**26, transcendentals=0),
        name="gather_keys_values",
    )(in_hbm(keys.reshape(2, ST, HD)), in_hbm(values.reshape(2, ST, HD)))
    bufs = [pltpu.VMEM((n, ST, HD), BF16) for n in SCATTER_BUFS]
    wide = jax.ShapeDtypeStruct((tok, HQ * HD), BF16)
    results = pl.pallas_call(
        attend_scatter_kernel,
        out_shape=(wide, wide, own, own),
        in_specs=[smem] * 2 + [vmem] * 5,
        out_specs=(vmem, hbm, vmem, vmem),
        scratch_shapes=[
            pltpu.SMEM((RANKS,), jnp.int32),
            pltpu.VMEM((ROWS, HD), BF16),
            pltpu.VMEM((ROWS, HD), BF16),
            pltpu.VMEM((WIN * ST, HD), BF16),
            pltpu.VMEM((WIN * ST, HD), BF16),
            pltpu.VMEM((CHUNKS, CHUNK, ROWS), F32),
            pltpu.VMEM((2, WIN + 1, ST, HD), F32),
            pltpu.VMEM((2, WIN + 1, ST, HD), F32),
        ]
        + bufs
        + bufs
        + [dma((19,))] * 4
        + [dma((2,))],
        compiler_params=pltpu.CompilerParams(collective_id=1, has_side_effects=True, vmem_limit_bytes=28 << 20),
        cost_estimate=pl.CostEstimate(flops=2**33, bytes_accessed=2**26, transcendentals=0),
        name="attend_scatter",
    )(in_hbm(doc_lengths), in_hbm(pair_of_rank), queries[0], attn_out[0], grad_out[0], all_keys, all_values)
    query_grad, handed, key_grad, value_grad = pl.pallas_call(
        finish_kernel,
        out_shape=(wide, wide, own, own),
        in_specs=[vmem] * 4,
        out_specs=(vmem,) * 4,
        compiler_params=pltpu.CompilerParams(vmem_limit_bytes=4 << 20),
        name="finish",
    )(*results)
    return (
        query_grad[None],
        handed[None],
        key_grad.reshape(1, tok, HD),
        value_grad.reshape(1, tok, HD),
    )


def solution(mesh):
    split = P("pipe", "ctx", None)
    return jax.shard_map(
        on_device,
        mesh=mesh,
        in_specs=(split,) * 5 + (P(), P()),
        out_specs=(split,) * 4,
        check_vma=False,
    )
```

```python
import math

import jax
import jax.numpy as jnp
from jax import lax
from jax.experimental import pallas as pl
from jax.experimental.pallas import tpu as pltpu
from jax.sharding import PartitionSpec as P

HQ = 8
HD = 128
ST = 64
RANKS = 32
SIDE = 4
STRETCHES = 2 * RANKS
WIN = 18
CHUNK = 384
PART = CHUNK // ST
CHUNKS = WIN * ST // CHUNK
ROWS = HQ * ST
GROUP = 2 * SIDE
NEG = -1e30
MESH = pl.DeviceIdType.MESH
F32 = jnp.float32
BF16 = jnp.bfloat16


class Place:
    def __init__(self):
        me = lax.axis_index("ctx")
        self.core = lax.rem(me, 2)
        chip = me // 2
        self.x = lax.rem(chip, SIDE)
        self.y = chip // SIDE

    def at(self, dx, dy):
        x = lax.rem(self.x + dx + SIDE, SIDE)
        y = lax.rem(self.y + dy + SIDE, SIDE)
        return (y * SIDE + x) * 2 + self.core

    def sibling(self):
        return (self.y * SIDE + self.x) * 2 + 1 - self.core

    def neighbours(self):
        steps = [(1, 0), (-1, 0), (2, 0), (0, 1), (0, -1), (0, 2)]
        return [self.sibling()] + [self.at(dx, dy) for dx, dy in steps]

    def order(self, fast_is_x):
        if fast_is_x:
            return self.x, self.y, (lambda d: self.at(d, 0)), (lambda d: self.at(0, d))
        return self.y, self.x, (lambda d: self.at(0, d)), (lambda d: self.at(d, 0))


def step(i, d):
    return lax.rem(i + d + SIDE, SIDE)


def in_turn(*streams):
    live = list(streams)
    while live:
        for stream in list(live):
            if next(stream, StopIteration) is StopIteration:
                live.remove(stream)


def sender(send_sem, recv_sem):
    sent = {}

    def send(i, src, dst, device):
        copy = pltpu.make_async_remote_copy(
            src_ref=src, dst_ref=dst, send_sem=send_sem.at[i], recv_sem=recv_sem.at[i],
            device_id={"ctx": device}, device_id_type=MESH,
        )
        copy.start()
        sent[i] = copy

    return sent, send


def gather_stream(place, fast_is_x, own, full, own_sem, send_sem, recv_sem):
    fast, slow, along_fast, along_slow = place.order(fast_is_x)
    sent, send = sender(send_sem, recv_sem)
    half = place.core * (SIDE * GROUP)

    def block(f, d=0):
        return full.at[pl.ds(half + step(slow, d) * GROUP + step(fast, f) * 2, 2)]

    def group(d):
        return full.at[pl.ds(half + step(slow, d) * GROUP, GROUP)]

    def spread(i, f, src=None):
        src = block(f) if src is None else src
        send(i, src, block(f), along_slow(1))
        send(i + 1, src, block(f), along_slow(-1))

    def relay(i, f, toward):
        send(i, block(f, -toward), block(f, -toward), along_slow(toward))

    send(0, own, block(0), along_fast(1))
    send(1, own, block(0), along_fast(-1))
    send(2, own, block(0), along_fast(2))
    spread(4, 0, own)
    mine = pltpu.make_async_copy(own, block(0), own_sem)
    mine.start()
    yield
    sent[0].wait_recv()
    spread(6, -1)
    yield
    sent[1].wait_recv()
    spread(8, 1)
    yield
    sent[4].wait_recv()
    relay(12, 0, 1)
    yield
    sent[2].wait_recv()
    spread(10, 2)
    send(15, block(2), block(2), along_slow(2))
    mine.wait()
    send(16, group(0), group(0), place.sibling())
    yield
    sent[7].wait_recv()
    relay(13, -1, -1)
    yield
    sent[9].wait_recv()
    relay(14, 1, -1)
    yield
    sent[6].wait_recv()
    sent[8].wait_recv()
    sent[10].wait_recv()
    send(17, group(-1), group(-1), place.sibling())
    yield
    sent[5].wait_recv()
    sent[11].wait_recv()
    send(18, group(1), group(1), place.sibling())
    yield
    for n, f in enumerate((0, -1, 1, 2)):
        sent[12 + n].wait_recv()
        send(19 + n, block(f, 2), block(f, 2), place.sibling())
        yield
    for i in range(16, 23):
        sent[i].wait_recv()
    for copy in sent.values():
        copy.wait_send()


def gather_kernel(k_ref, v_ref, gk_ref, gv_ref, own_sem, k_send, k_recv, v_send, v_recv):
    place = Place()
    barrier = pltpu.get_barrier_semaphore()
    for device in place.neighbours():
        pl.semaphore_signal(barrier, inc=1, device_id={"ctx": device}, device_id_type=MESH)
    pl.semaphore_wait(barrier, 7)
    in_turn(
        gather_stream(place, True, k_ref, gk_ref, own_sem.at[0], k_send, k_recv),
        gather_stream(place, False, v_ref, gv_ref, own_sem.at[1], v_send, v_recv),
    )


def add(*terms):
    total = terms[0].astype(F32)
    for term in terms[1:]:
        total = total + term.astype(F32)
    return total.astype(BF16)


def scatter_stream(place, fast_is_x, term, out, bufs, send_sem, recv_sem):
    outgoing, sib, acc, across, from_low, from_high, line, far, end_low, end_high = bufs
    fast, slow, along_fast, along_slow = place.order(fast_is_x)
    sent, send = sender(send_sem, recv_sem)
    order = (2, 1, -1, 0)
    way = (1, -1, -1, 1)

    def at(d):
        return pl.ds(step(slow, d) * GROUP, GROUP)

    def block(d, n):
        return pl.ds(step(slow, d) * GROUP + step(fast, order[n]) * 2, 2)

    def slot(n):
        return pl.ds(2 * n, 2)

    def own_term(core, d, n):
        line_at, half = step(slow, d), n % 2
        y, x = (line_at, n // 2) if fast_is_x else (n // 2, line_at)
        return term((y * SIDE + x) * 2 + core, half)

    def own_terms(core, d):
        return jnp.stack([own_term(core, d, n) for n in range(GROUP)])

    def prepare(d):
        acc[at(d)] = own_terms(place.core, d)

    def merge(d):
        acc[at(d)] = add(acc[at(d)], sib[at(d)])

    for i, d in enumerate((2, 1, -1, 0)):
        outgoing[at(d)] = own_terms(1 - place.core, d)
        send(i, outgoing.at[at(d)], sib.at[at(d)], place.sibling())
        yield
    prepare(2)
    yield
    sent[0].wait_recv()
    merge(2)
    for n in range(4):
        send(4 + n, acc.at[block(2, n)], across.at[slot(n)], along_slow(way[n] if n else 2))
    prepare(1)
    yield
    sent[1].wait_recv()
    merge(1)
    send(12, acc.at[block(1, 0)], from_low.at[slot(0)], along_slow(1))
    for n in (1, 2):
        send(8 + n, acc.at[block(1, n)], from_low.at[slot(n)], along_slow(1))
    prepare(-1)
    yield
    sent[2].wait_recv()
    merge(-1)
    for n in (0, 3):
        send(8 + n, acc.at[block(-1, n)], from_high.at[slot(n)], along_slow(-1))
    prepare(0)
    yield
    sent[3].wait_recv()
    merge(0)
    yield
    def settle(n, *more):
        sent[8 + n].wait_recv()
        sent[12 + n].wait_recv()
        line[slot(n)] = add(acc[block(0, n)], from_low[slot(n)], from_high[slot(n)], *more)

    for n in range(1, 4):
        sent[4 + n].wait_recv()
        acc[block(way[n], n)] = add(acc[block(way[n], n)], across[slot(n)])
        target = from_low if way[n] == 1 else from_high
        send(12 + n, acc.at[block(way[n], n)], target.at[slot(n)], along_slow(way[n]))
        yield
    sent[4].wait_recv()
    settle(0, across[slot(0)])
    send(16, line.at[slot(0)], far, along_fast(2))
    yield
    settle(1)
    send(17, line.at[slot(1)], end_low, along_fast(1))
    yield
    settle(2)
    send(18, line.at[slot(2)], end_high, along_fast(-1))
    yield
    settle(3)
    for i in (16, 17, 18):
        sent[i].wait_recv()
    out[...] = add(line[slot(3)], end_low[...], end_high[...], far[...])
    for copy in sent.values():
        copy.wait_send()


SCATTER_BUFS = (SIDE * GROUP, SIDE * GROUP, SIDE * GROUP, GROUP, GROUP, GROUP, GROUP, 2, 2, 2)


def dot(a, b, over):
    return lax.dot_general(a, b, ((over[:1], over[1:]), ((), ())), preferred_element_type=F32)


def attend_scatter_kernel(
    docs, pairs, q_ref, o_ref, g_ref, k_ref, v_ref, dq_ref, handed_ref, kg_ref, vg_ref,
    rank_of_pair, q_rows, g_rows, key_win, value_win, work, key_terms, value_terms, *scratch,
):
    count = len(SCATTER_BUFS)
    k_bufs, v_bufs = scratch[:count], scratch[count : 2 * count]
    k_send, k_recv, v_send, v_recv, hand_sem = scratch[2 * count :]
    place = Place()
    section, sections = lax.axis_index("pipe"), lax.axis_size("pipe")
    below = lax.rem(section + sections - 1, sections)
    above = lax.rem(section + 1, sections)
    barrier = pltpu.get_barrier_semaphore()
    for device in place.neighbours():
        pl.semaphore_signal(barrier, inc=1, device_id={"ctx": device}, device_id_type=MESH)
    for device in (below, above):
        pl.semaphore_signal(barrier, inc=1, device_id={"pipe": device}, device_id_type=MESH)
    scale = 1.0 / math.sqrt(HD)
    pair = pairs[lax.axis_index("ctx")]

    def note(p, carry):
        found = jnp.int32(0)
        for r in range(RANKS):
            found = jnp.maximum(found, jnp.where(pairs[r] == p, r, 0))
        rank_of_pair[p] = found
        return carry

    lax.fori_loop(0, RANKS, note, 0)

    def places(t):
        late = (t >= RANKS).astype(jnp.int32)
        rank = rank_of_pair[jnp.where(t >= RANKS, STRETCHES - 1 - t, t)]
        core, chip = lax.rem(rank, 2), rank // 2
        turned = lax.rem(chip, SIDE) * SIDE + chip // SIDE
        size = SIDE * SIDE
        return (core * size + chip) * 2 + late, (core * size + turned) * 2 + late

    for which in range(2):
        key_terms[which, WIN] = jnp.zeros((ST, HD), F32)
        value_terms[which, WIN] = jnp.zeros((ST, HD), F32)
    bases = (pair, STRETCHES - 1 - pair)
    lane = lax.rem(lax.broadcasted_iota(jnp.int32, (1, ROWS), 1), ST)
    for which in range(2):
        base = bases[which]
        lowest = (base - (WIN - 1)) * ST
        rows = slice(which * ST, (which + 1) * ST)
        for h in range(HQ):
            q_rows[h * ST : (h + 1) * ST] = q_ref[rows, h * HD : (h + 1) * HD]
            g_rows[h * ST : (h + 1) * ST] = g_ref[rows, h * HD : (h + 1) * HD]
        products = jnp.concatenate(
            [
                g_ref[rows, h * HD : (h + 1) * HD].astype(F32) * o_ref[rows, h * HD : (h + 1) * HD].astype(F32)
                for h in range(HQ)
            ],
            axis=0,
        )
        delta = jnp.sum(jnp.transpose(products), axis=0, keepdims=True)
        for j in range(WIN):
            k_at, v_at = places(jnp.maximum(base - (WIN - 1) + j, 0))
            key_win[j * ST : (j + 1) * ST] = k_ref[k_at]
            value_win[j * ST : (j + 1) * ST] = v_ref[v_at]
        position = base * ST + lane
        start, end = jnp.zeros_like(position), jnp.int32(0)
        for d in range(docs.shape[0]):
            end = end + docs[d]
            start = jnp.where(position >= end, end, start)
        low, high = start - lowest, position - lowest

        def scores(c, top):
            at = pl.multiple_of(c * CHUNK, CHUNK)
            found = dot(key_win[pl.ds(at, CHUNK)], q_rows[...], (1, 1))
            where = lax.broadcasted_iota(jnp.int32, (CHUNK, ROWS), 0) + at
            found = jnp.where((where >= low) & (where <= high), found, NEG)
            work[c] = found
            return jnp.maximum(top, jnp.max(found, axis=0, keepdims=True))

        top = lax.fori_loop(0, CHUNKS, scores, jnp.full((1, ROWS), NEG, F32))

        def weigh(c, total):
            weights = jnp.exp2((work[c] - top) * (scale * math.log2(math.e)))
            work[c] = weights
            return total + jnp.sum(weights, axis=0, keepdims=True)

        total = lax.fori_loop(0, CHUNKS, weigh, jnp.zeros((1, ROWS), F32))
        inverse = 1.0 / total

        def grads(c, dq_sum):
            at = pl.multiple_of(c * CHUNK, CHUNK)
            probs = work[c] * inverse
            value_terms[which, pl.ds(c * PART, PART)] = dot(probs.astype(BF16), g_rows[...], (1, 0)).reshape(PART, ST, HD)
            dprobs = dot(value_win[pl.ds(at, CHUNK)], g_rows[...], (1, 1))
            dscores = (probs * (dprobs - delta)).astype(BF16)
            key_terms[which, pl.ds(c * PART, PART)] = (dot(dscores, q_rows[...], (1, 0)) * scale).reshape(PART, ST, HD)
            turned = jnp.transpose(key_win[pl.ds(at, CHUNK)])
            return dq_sum + dot(turned, dscores, (1, 0))

        dq_sum = lax.fori_loop(0, CHUNKS, grads, jnp.zeros((HD, ROWS), F32))
        dq_rows = (jnp.transpose(dq_sum) * scale).astype(BF16)
        for h in range(HQ):
            dq_ref[rows, h * HD : (h + 1) * HD] = dq_rows[h * ST : (h + 1) * ST]

    early, late = bases[0] - (WIN - 1), bases[1] - (WIN - 1)

    def within(j):
        return jnp.where((j >= 0) & (j < WIN), j, WIN)

    def term_of(terms):
        def term(rank, half):
            t = pairs[rank] if half == 0 else STRETCHES - 1 - pairs[rank]
            return (terms[0, within(t - early)] + terms[1, within(t - late)]).astype(BF16)

        return term

    pl.semaphore_wait(barrier, 9)
    hand = pltpu.make_async_remote_copy(
        src_ref=dq_ref, dst_ref=handed_ref, send_sem=hand_sem.at[0], recv_sem=hand_sem.at[1],
        device_id={"pipe": below}, device_id_type=MESH,
    )
    hand.start()
    in_turn(
        scatter_stream(place, True, term_of(key_terms), kg_ref, k_bufs, k_send, k_recv),
        scatter_stream(place, False, term_of(value_terms), vg_ref, v_bufs, v_send, v_recv),
    )
    hand.wait()


def finish_kernel(*refs):
    for source, target in zip(refs[:4], refs[4:]):
        target[...] = source[...]


def in_hbm(x):
    return pltpu.with_memory_space_constraint(x, pltpu.HBM)


def on_device(queries, keys, values, attn_out, grad_out, doc_lengths, pair_of_rank):
    vmem = pl.BlockSpec(memory_space=pltpu.VMEM)
    smem = pl.BlockSpec(memory_space=pltpu.SMEM)
    hbm = pl.BlockSpec(memory_space=pl.ANY)
    full = jax.ShapeDtypeStruct((STRETCHES, ST, HD), BF16)
    own = jax.ShapeDtypeStruct((2, ST, HD), BF16)
    tok = 2 * ST
    dma = pltpu.SemaphoreType.DMA
    all_keys, all_values = pl.pallas_call(
        gather_kernel,
        out_shape=(full, full),
        in_specs=[pl.BlockSpec(memory_space=pltpu.HBM)] * 2,
        out_specs=(vmem, vmem),
        scratch_shapes=[dma((2,))] + [dma((23,))] * 4,
        compiler_params=pltpu.CompilerParams(collective_id=0, has_side_effects=True, vmem_limit_bytes=8 << 20),
        cost_estimate=pl.CostEstimate(flops=2**33, bytes_accessed=2**26, transcendentals=0),
        name="gather_keys_values",
    )(in_hbm(keys.reshape(2, ST, HD)), in_hbm(values.reshape(2, ST, HD)))
    bufs = [pltpu.VMEM((n, ST, HD), BF16) for n in SCATTER_BUFS]
    wide = jax.ShapeDtypeStruct((tok, HQ * HD), BF16)
    results = pl.pallas_call(
        attend_scatter_kernel,
        out_shape=(wide, wide, own, own),
        in_specs=[smem] * 2 + [vmem] * 5,
        out_specs=(vmem, hbm, vmem, vmem),
        scratch_shapes=[
            pltpu.SMEM((RANKS,), jnp.int32),
            pltpu.VMEM((ROWS, HD), BF16),
            pltpu.VMEM((ROWS, HD), BF16),
            pltpu.VMEM((WIN * ST, HD), BF16),
            pltpu.VMEM((WIN * ST, HD), BF16),
            pltpu.VMEM((CHUNKS, CHUNK, ROWS), F32),
            pltpu.VMEM((2, WIN + 1, ST, HD), F32),
            pltpu.VMEM((2, WIN + 1, ST, HD), F32),
        ]
        + bufs
        + bufs
        + [dma((19,))] * 4
        + [dma((2,))],
        compiler_params=pltpu.CompilerParams(collective_id=1, has_side_effects=True, vmem_limit_bytes=28 << 20),
        cost_estimate=pl.CostEstimate(flops=2**33, bytes_accessed=2**26, transcendentals=0),
        name="attend_scatter",
    )(in_hbm(doc_lengths), in_hbm(pair_of_rank), queries[0], attn_out[0], grad_out[0], all_keys, all_values)
    query_grad, handed, key_grad, value_grad = pl.pallas_call(
        finish_kernel,
        out_shape=(wide, wide, own, own),
        in_specs=[vmem] * 4,
        out_specs=(vmem,) * 4,
        compiler_params=pltpu.CompilerParams(vmem_limit_bytes=4 << 20),
        name="finish",
    )(*results)
    return (
        query_grad[None],
        handed[None],
        key_grad.reshape(1, tok, HD),
        value_grad.reshape(1, tok, HD),
    )


def solution(mesh):
    split = P("pipe", "ctx", None)
    return jax.shard_map(
        on_device,
        mesh=mesh,
        in_specs=(split,) * 5 + (P(), P()),
        out_specs=(split,) * 4,
        check_vma=False,
    )
```
